128 devices in a mesh: det: 8 (over y, core), tm: 16 (over z, x).
Axes of the slice: x: 4, y: 4, z: 4, core: 2. Of those that a mesh axis runs over, the one named last changes fastest.
Arguments:
- detector_data: float32 [512, 131072], P('det', 'tm'), may hold values from -6 to 6
- sky_map: float32 [4096, 8192], P(('det', 'tm')), may hold values from -6 to 6
- pointing: int32 [512, 1024], P('det', 'tm'), may hold values from 0 to 511
- request_owner: int32 [2048, 1], P(('det', 'tm')), may hold values from 0 to 15; in each aligned block of 16 rows (0 to 15, 16 to 31, ...) at most 2 rows name the same one
- request_block: int32 [2048], P(('det', 'tm')), may hold values from 0 to 63
- beam_kernel: float32 [128, 128], replicated, may hold values from -0.5 to 0.5
- inv_white: float32 [512, 32], P('det'), may hold values from 0.5 to 4
- mode_loading: float32 [512, 16], P('det'), may hold values from -1 to 1
- mode_kernel: float32 [32, 16, 16], replicated, may hold values from -0.75 to 0.75
Outputs:
- map_gradient: float32 [4096, 8192], P(('det', 'tm'))
The draws below stay inside these ranges and needn't reach their ends.
Inputs may be any that keep to these rules, and one draw needn't show every extreme that they name: `request_owner`: among the 16 requests of one device, no owner is named more than 2 times, and in every draw some device names some owner exactly 2 times.
All inputs are finite; a program needn't handle non-finite values.
Results may differ from the reference program's by a relative error of at most 0.0003.
Values sent between devices are 32-bit elements; how exact they have to be, the bound alone decides.
No kernel may reach another device: no remote copies, remote signals or barrier semaphores. Data moves between devices by JAX's collectives and lax.ppermute only.
A program may use at most 256 MiB of HBM per device.

```python
import math
import jax
import jax.numpy as jnp
import numpy as np
from jax import lax

DET_DEV = 64
SAMPLES = 8192
TILE = 128
MODES = 16
NBAND = 32
BANDW = 128
LIST = 16
NY = 4096
NX = 8192
NDET = 512
NSAMP = 131072
BROWS = 32
BPD = 64
CAP = 2
NTILE = 64
N_DET = 8
N_TM = 16
DEVICES = 128


def draw_sky_map(key, part):
    phase_key = jax.random.fold_in(key, 11)
    second_key = jax.random.fold_in(key, 12)
    noise_key = jax.random.fold_in(key, 13)
    row_index = jnp.arange(NY, dtype=jnp.int32)[:, None]
    first_turn = (row_index * 255 % 512).astype(jnp.float32) * (2.0 * math.pi / 512.0)
    second_turn = (row_index * 15 % 32).astype(jnp.float32) * (2.0 * math.pi / 32.0)
    first_phase = jax.random.uniform(phase_key, (1, NX), jnp.float32, -math.pi, math.pi)
    second_phase = jax.random.uniform(second_key, (1, NX), jnp.float32, -math.pi, math.pi)
    amplitudes = jnp.full((2, 1, NX), 3.0, jnp.float32)
    noise = 0.7 * jax.random.normal(noise_key, (NY, NX), jnp.float32)
    waves = amplitudes[0] * jnp.cos(first_turn + first_phase) + amplitudes[1] * jnp.cos(second_turn + second_phase)
    return jnp.clip(waves + noise, -6.0, 6.0).astype(jnp.float32)


def place_ends(array, rng, low, high):
    spot = [jax.random.randint(jax.random.fold_in(rng, axis), (), 0, length) for axis, length in enumerate(array.shape)]
    widest = array.shape.index(max(array.shape))
    next_to = spot[:widest] + [(spot[widest] + 1) % array.shape[widest]] + spot[widest + 1:]
    return array.at[tuple(spot)].set(low).at[tuple(next_to)].set(high)


def block_scale(key, shape, split, low, high):
    level, own = 1.0, jax.random.fold_in(key, 6)
    for axis_at, parts in split:
        draws = jnp.exp(jax.random.uniform(jax.random.fold_in(own, axis_at), (parts,), jnp.float32, low / len(split), high / len(split)))
        level = level * jnp.repeat(draws, shape[axis_at] // parts).reshape([-1 if axis == axis_at else 1 for axis in range(len(shape))])
    return level


def routed_block(rng, own, number, rows, amount, top, limit, slope):
    ranking = jax.random.permutation(rng, amount)
    crowded, ordinary = load_shares(amount, rows * top, limit, slope, True), load_shares(amount, rows * top, limit, slope, False)
    places = jnp.arange(amount)

    def named(lengths, rotation):
        used = int((lengths > 0).sum())
        fixed = max(1, used // 4)
        passed = fixed + (places - fixed + rotation * (used - fixed)) % max(1, amount - fixed)
        return jnp.zeros((amount,), jnp.int32).at[ranking[jnp.where(places < fixed, places, passed)]].set(jnp.asarray(lengths, jnp.int32))

    lengths = jnp.where(number % 4 == 0, named(crowded, number // 4), named(ordinary, number - number // 4 - 1))
    mixed = jax.random.permutation(jax.random.fold_in(own, 3), amount)
    giver, taker = mixed[0:amount // 2 * 2:2], mixed[1:amount // 2 * 2:2]
    margin = jnp.minimum(lengths[giver] - 1, limit - lengths[taker]) // 2
    margin = jnp.where((giver == ranking[0]) | (taker == ranking[0]) | (lengths[taker] == 0), 0, jnp.maximum(margin, 0))
    passed = jax.random.randint(jax.random.fold_in(own, 4), (amount // 2,), 0, 1 << 20) % (margin + 1)
    lengths = lengths.at[giver].add(-passed).at[taker].add(passed)
    items = jnp.searchsorted(jnp.cumsum(lengths), jnp.arange(rows * top), side="right").astype(jnp.int32)
    grid = items.reshape(top, rows).T
    grid = grid[jax.random.permutation(jax.random.fold_in(own, 1), rows)]
    rotation = jax.random.randint(jax.random.fold_in(own, 2), (rows, 1), 0, top)
    return jnp.take_along_axis(grid, (jnp.arange(top)[None, :] + rotation) % top, axis=1)


def load_shares(number_of, total, reach, slope, full):
    weights = [(1 << 20) // math.isqrt(rank ** slope) + 1 for rank in range(1, number_of + 1)]
    largest = reach if full else min(reach, max(-(-total // number_of), total * weights[0] // sum(weights)))
    least = 1 if total - largest >= number_of - 1 else 0
    counts, surplus = [largest] + [least] * (number_of - 1), total - largest - least * (number_of - 1)
    while surplus > 0:
        candidates = [i for i in range(1, number_of) if counts[i] < largest] or [i for i in range(1, number_of) if counts[i] < reach]
        pool, left = sum([weights[i] for i in candidates]), surplus
        for i in candidates:
            more = min(reach - counts[i], max(1, left * weights[i] // pool), surplus)
            counts[i] = counts[i] + more
            surplus = surplus - more
    return np.array(counts)


def scatter_about(key, dims, width, most, split=(), held_as=jnp.bfloat16):
    values = jax.random.normal(key, dims, jnp.float32) * width
    if len(split) > 0:
        values = block_scale(key, dims, split, -0.22, 0.18) * values
    return jnp.clip(values, min=-most, max=most).astype(held_as)


def setup_inputs(seed: int = 0) -> dict:
    seeds = jax.random.split(jax.random.key(seed), 10)
    detector_data = scatter_about(seeds[0], (NDET, NSAMP), 1.0, 6.0, ((0, 8), (1, 16)), jnp.float32)
    sky_map = draw_sky_map(jax.random.fold_in(seeds[9], 71), 0)
    pointing = place_ends(jax.random.randint(seeds[2], (NDET, NSAMP // TILE), 0, LIST * BROWS), jax.random.fold_in(seeds[2], 1), 0, (LIST * BROWS) - 1).astype(jnp.int32)
    request_owner_keys = jax.random.split(jax.random.fold_in(seeds[3], 1), (DEVICES * LIST) // LIST)
    request_owner_turns = jax.random.permutation(jax.random.fold_in(seeds[3], 3), (DEVICES * LIST) // LIST)
    request_owner = jax.vmap(lambda own, number: routed_block(jax.random.fold_in(seeds[3], 2), own, number, LIST, N_TM, 1, CAP, 2))(request_owner_keys, request_owner_turns).reshape((DEVICES * LIST, 1))
    request_block = place_ends(jax.random.randint(seeds[4], (DEVICES * LIST,), 0, BPD), jax.random.fold_in(seeds[4], 1), 0, BPD - 1).astype(jnp.int32)
    beam_kernel = scatter_about(seeds[5], (TILE, TILE), TILE ** -0.5, 0.5, (), jnp.float32)
    inv_white = jnp.clip(jnp.exp(math.log(4.0) - 2.0794415 * jax.random.uniform(seeds[6], (NDET, NBAND), jnp.float32) ** block_scale(seeds[6], (NDET, NBAND), ((0, 8),), -0.2, 0.2)), 0.5, 4.0)
    mode_loading = scatter_about(seeds[7], (NDET, MODES), (max(NDET // 16, 1)) ** -0.5, 1.0, ((0, 8),), jnp.float32)
    mode_kernel = scatter_about(seeds[8], (NBAND, MODES, MODES), (4 * MODES) ** -0.5, 0.75, (), jnp.float32)
    return {"detector_data": detector_data, "sky_map": sky_map, "pointing": pointing, "request_owner": request_owner, "request_block": request_block, "beam_kernel": beam_kernel, "inv_white": inv_white, "mode_loading": mode_loading, "mode_kernel": mode_kernel}


precise = lax.Precision.HIGHEST

def prior_gain(vertical, horizontal, total_rows, total_cols):
    fold_rows = jnp.minimum(vertical, total_rows - vertical).astype(jnp.float32) / total_rows
    fold_cols = jnp.minimum(horizontal, total_cols - horizontal).astype(jnp.float32) / total_cols
    radial_sq = fold_rows * fold_rows + fold_cols * fold_cols
    length_scale = total_rows / 64.0
    knee_sq = 1.0 / (2.0 * math.pi * length_scale) ** 2
    return 1.0 + radial_sq / 0.05 + 0.25 / jnp.sqrt(radial_sq + knee_sq)

def reference(detector_data, sky_map, pointing, request_owner, request_block, beam_kernel, inv_white, mode_loading, mode_kernel):
    sky_grid = sky_map.reshape(NY, BPD, TILE)
    owner_all = request_owner[:, 0].reshape(N_DET, N_TM, LIST)
    block_all = request_block.reshape(N_DET, N_TM, LIST)
    frequency = jnp.arange(SAMPLES, dtype=jnp.int32)
    folded = jnp.minimum(frequency, SAMPLES - frequency)
    band_index = jnp.minimum(folded // BANDW, NBAND - 1)
    weight_freq = inv_white[:, band_index]
    kernel_freq = mode_kernel[band_index]
    det_group = (jnp.arange(NDET, dtype=jnp.int32) // DET_DEV)[:, None]

    def per_segment(gradient_grid, segment):
        data_now = lax.dynamic_slice_in_dim(detector_data, segment * SAMPLES, SAMPLES, 1)
        tiles_now = lax.dynamic_slice_in_dim(pointing, segment * NTILE, NTILE, 1)
        list_slot = tiles_now // BROWS
        block_row = tiles_now % BROWS
        owner_tm = owner_all[det_group, segment, list_slot]
        block_col = block_all[det_group, segment, list_slot]
        map_row = (det_group * N_TM + owner_tm) * BROWS + block_row
        sky_rows = sky_grid[map_row, block_col]
        signal = jnp.einsum('jsp,ip->jsi', sky_rows, beam_kernel, precision=precise).reshape(NDET, SAMPLES)
        spectrum = jnp.fft.fft(data_now - signal, axis=1)
        spec_real = jnp.real(spectrum)
        spec_imag = jnp.imag(spectrum)
        proj_real = jnp.einsum('jm,jf->mf', mode_loading, weight_freq * spec_real, precision=precise)
        proj_imag = jnp.einsum('jm,jf->mf', mode_loading, weight_freq * spec_imag, precision=precise)
        coupled_real = jnp.einsum('fmn,nf->mf', kernel_freq, proj_real, precision=precise)
        coupled_imag = jnp.einsum('fmn,nf->mf', kernel_freq, proj_imag, precision=precise)
        filt_real = weight_freq * (spec_real - jnp.einsum('jm,mf->jf', mode_loading, coupled_real, precision=precise))
        filt_imag = weight_freq * (spec_imag - jnp.einsum('jm,mf->jf', mode_loading, coupled_imag, precision=precise))
        cleaned = jnp.real(jnp.fft.ifft(lax.complex(filt_real, filt_imag), axis=1))
        tile_grads = jnp.einsum('jsi,ip->jsp', cleaned.reshape(NDET, NTILE, TILE), beam_kernel, precision=precise)
        gradient_grid = gradient_grid.at[map_row, block_col].add(tile_grads)
        return (gradient_grid, None)
    start_grid = jnp.zeros((NY, BPD, TILE), jnp.float32)
    gradient_grid = lax.scan(per_segment, start_grid, jnp.arange(N_TM, dtype=jnp.int32))[0]
    map_spectrum = jnp.fft.fft2(sky_map)
    gain_grid = prior_gain(jnp.arange(NY, dtype=jnp.int32)[:, None], jnp.arange(NX, dtype=jnp.int32)[None, :], NY, NX)
    prior_term = jnp.real(jnp.fft.ifft2(map_spectrum * gain_grid))
    return gradient_grid.reshape(NY, NX) - prior_term
```

```python
import math

import jax
import jax.numpy as jnp
import numpy as np
from jax import lax
from jax.experimental import pallas as pl
from jax.experimental.pallas import tpu as pltpu
from jax.sharding import PartitionSpec as P

NBAND = 32
F32 = jnp.float32
BF16 = jnp.bfloat16
VM = pltpu.VMEM


def halves(table):
    high = np.asarray(table, np.float32).astype(BF16)
    low = (np.asarray(table, np.float64) - high.astype(np.float64)).astype(BF16)
    return high, low


def wave(rows, cols, period):
    turn = 2.0 * math.pi * ((rows[:, None] * cols[None, :]) % period) / period
    return np.cos(turn), np.sin(turn)


def stage_tables(width, copies):
    index = np.arange(width, dtype=np.float64)
    cos, sin = wave(index, index, width)
    half_cos, half_sin = wave(index, index + 0.5, width)
    eye = np.eye(copies)
    cos, sin = np.kron(eye, cos), np.kron(eye, sin)
    cas_half = np.kron(eye, half_cos + half_sin)
    zero = np.zeros_like(cos)
    general = np.block([[cos, -sin], [sin, cos]])
    special = np.block([[cos + sin, zero], [zero, cas_half]])
    return general, special


def row_tables():
    general, special = stage_tables(128, 1)
    return general, special


def twiddles(first, second, length):
    return [
        np.asarray(t, np.float32)
        for t in wave(np.arange(first, dtype=np.float64), second.astype(np.float64), length)
    ]


def real_left_table():
    index = np.arange(64, dtype=np.float64)
    cos, sin = wave(index, np.arange(128, dtype=np.float64), 128)
    forward = np.concatenate([cos, -sin], axis=0)
    forward[64] = np.cos(math.pi * np.arange(128))
    inverse = 2.0 * forward.T
    inverse[:, 0] = 1.0
    inverse[:, 64] = forward[64]
    return forward, inverse


def band_tables():
    second = np.arange(128)
    general = np.minimum(np.minimum(second, 127 - second) // 2, NBAND - 1)
    special = np.minimum(np.minimum(second, 128 - second) // 2, NBAND - 1)
    bands = np.arange(NBAND)[:, None]
    return (bands == general[None]).astype(np.float32), (bands == special[None]).astype(np.float32)


def turn_by(pair, quotient, count, sign):
    real, imag = pair
    cos = math.cos(2.0 * math.pi * quotient / count)
    sin = sign * math.sin(2.0 * math.pi * quotient / count)
    if 8 * quotient == count:
        scale = math.sqrt(0.5)
        if sign < 0:
            return (real + imag) * scale, (imag - real) * scale
        return (real - imag) * scale, (imag + real) * scale
    return real * cos - imag * sin, real * sin + imag * cos


def real_transform(values):
    count = len(values)
    if count == 1:
        return [(values[0], None)]
    if count == 2:
        return [(values[0] + values[1], None), (values[0] - values[1], None)]
    even = real_transform(values[0::2])
    odd = real_transform(values[1::2])
    half = count // 2
    out = [None] * (half + 1)
    out[0] = (even[0][0] + odd[0][0], None)
    out[half] = (even[0][0] - odd[0][0], None)
    for k in range(1, half // 2):
        turned = turn_by(odd[k], k, count, -1.0)
        out[k] = (even[k][0] + turned[0], even[k][1] + turned[1])
        out[half - k] = (even[k][0] - turned[0], turned[1] - even[k][1])
    out[half // 2] = (even[half // 2][0], -odd[half // 2][0])
    return out


def real_inverse(spectrum, count):
    if count == 1:
        return [spectrum[0][0]]
    first, last = spectrum[0][0], spectrum[count // 2][0]
    if count == 2:
        return [first + last, first - last]
    half = count // 2
    even = [None] * (half // 2 + 1)
    odd = [None] * (half // 2 + 1)
    even[0] = (first + last, None)
    odd[0] = (first - last, None)
    for k in range(1, half // 2):
        one, two = spectrum[k], spectrum[half - k]
        even[k] = (one[0] + two[0], one[1] - two[1])
        odd[k] = turn_by((one[0] - two[0], one[1] + two[1]), k, count, 1.0)
    middle = spectrum[half // 2]
    even[half // 2] = (middle[0] + middle[0], None)
    odd[half // 2] = (-(middle[1] + middle[1]), None)
    out = [None] * count
    out[0::2] = real_inverse(even, half)
    out[1::2] = real_inverse(odd, half)
    return out


def forward_tile(values, cos_ref, sin_ref, store):
    spectrum = real_transform(values)
    store(0, spectrum[0][0], spectrum[32][0])
    for k in range(1, 32):
        real, imag = spectrum[k]
        cos, sin = cos_ref[k : k + 1, :], sin_ref[k : k + 1, :]
        store(k, real * cos + imag * sin, imag * cos - real * sin)


def inverse_tile(load, cos_ref, sin_ref):
    first, last = load(0)
    spectrum = [(first, None)]
    for k in range(1, 32):
        real, imag = load(k)
        cos, sin = cos_ref[k : k + 1, :], sin_ref[k : k + 1, :]
        spectrum.append((real * cos - imag * sin, imag * cos + real * sin))
    spectrum.append((last, None))
    return real_inverse(spectrum, 64)


def parts(value):
    high = value.astype(BF16)
    return high, (value - high.astype(F32)).astype(BF16)


def mm(left, right):
    return jnp.dot(left, right, preferred_element_type=F32)


def mm_right(value, high, low):
    top, rest = parts(value)
    return mm(top, high) + mm(rest, high) + mm(top, low)


def mm_left(high, low, value):
    top, rest = parts(value)
    return mm(high, top) + mm(high, rest) + mm(low, top)


def mm_both(left, right):
    high, low = parts(right)
    return mm_right(left, high, low)


def aligned(index, size):
    return pl.ds(pl.multiple_of(index * size, size), size)


def ids_kernel(owner, block, send, slots, counts):
    for i in range(16):
        counts[i] = 0
    row = lax.broadcasted_iota(jnp.int32, (16, 128), 0)
    lane = lax.broadcasted_iota(jnp.int32, (16, 128), 1)
    table = jnp.full((16, 128), 64, jnp.int32)
    for i in range(16):
        target = owner[i]
        place = counts[target]
        counts[target] = place + 1
        slots[i] = target * 2 + place
        table = jnp.where((row == target) & (lane == place), block[i], table)
    send[...] = table


def pick_kernel(asked, sky, out):
    def step(i, carry):
        for c in range(2):
            block = jnp.minimum(asked[i, c], 63)
            out[2 * i + c] = sky[:, aligned(block, 128)]
        return carry

    lax.fori_loop(0, 16, step, 0)


def prep_kernel(inv_white, band, band_zero, kernel, weight, weight_zero, couple, couple_zero):
    for source, onehot, out in (
        (inv_white, band, weight),
        (inv_white, band_zero, weight_zero),
        (kernel, band, couple),
        (kernel, band_zero, couple_zero),
    ):
        out[...] = jnp.dot(
            source[...], onehot[...], precision=lax.Precision.HIGHEST, preferred_element_type=F32
        )


def rows_kernel(sky, cos, sin, gen_h, gen_l, spe_h, spe_l, out, work, done):
    def tile(i, carry):
        rows = aligned(i, 8)
        values = [sky[rows, 128 * u : 128 * u + 128] for u in range(64)]

        def store(k, real, imag):
            work[k, rows, 0:128] = real
            work[k, rows, 128:256] = imag

        forward_tile(values, cos, sin, store)
        return carry

    lax.fori_loop(0, 4, tile, 0)
    for q in range(2):
        chunk = work[16 * q : 16 * q + 16].reshape(512, 256)
        done[512 * q : 512 * q + 512] = mm_right(chunk, gen_h[...], gen_l[...])
    done[0:32] = mm_right(work[0], spe_h[...], spe_l[...])
    for t in range(8):
        for c in range(2):
            block = done[128 * t : 128 * t + 128, 128 * c : 128 * c + 128]
            out[:, 1024 * c + 128 * t : 1024 * c + 128 * t + 128] = block.T


def columns_kernel(
    rank, data, left_h, left_l, cos, sin, gen_h, gen_l, spe_h, spe_l, gent_h, gent_l, spet_h, spet_l,
    back_h, back_l, out, work, gained,
):
    for q in range(4):
        lanes = slice(512 * q, 512 * q + 512)
        both = mm_left(left_h[...], left_l[...], data[:, lanes])
        for s in range(4):
            t = 4 * q + s
            real, imag = both[0:64, 128 * s : 128 * s + 128], both[64:128, 128 * s : 128 * s + 128]
            work[t, :, 0:128] = real * cos[...] + imag * sin[...]
            work[t, :, 128:256] = imag * cos[...] - real * sin[...]
    total_rows, total_cols = 4096, 8192
    row = lax.broadcasted_iota(jnp.int32, (64, 128), 0)
    lane = lax.broadcasted_iota(jnp.int32, (64, 128), 1)
    squares = []
    for part in range(2):
        vertical = row + 128 * (lane % 32)
        if part:
            vertical = jnp.where(row == 0, 64 + 128 * (lane % 32), vertical)
        folded = jnp.minimum(vertical, total_rows - vertical).astype(F32) / total_rows
        squares.append(folded * folded)
    lane8 = lax.broadcasted_iota(jnp.int32, (8, 128), 1)
    base = rank[0] * 64
    knee_sq = 1.0 / (2.0 * math.pi * (total_rows / 64.0)) ** 2
    special = lax.broadcasted_iota(jnp.int32, (16, 8, 256), 1) == 0
    for q in range(2):
        tiles = slice(8 * q, 8 * q + 8)
        gained[tiles] = mm_right(
            work[tiles].reshape(512, 256), gen_h[...], gen_l[...]
        ).reshape(8, 64, 256)
    zero = mm_right(work[:, 0:8, :].reshape(128, 256), spe_h[...], spe_l[...]).reshape(16, 8, 256)
    gained[:, 0:8, :] = jnp.where(special, zero, gained[:, 0:8, :])

    def gain_tile(t, carry):
        first = 4 * (t % 8) + lane8 // 32
        first = jnp.where((first == 0) & (t == 8), 32, first)
        horizontal = base + first
        folded = jnp.minimum(horizontal, total_cols - horizontal).astype(F32) / total_cols
        across = (folded * folded)[0:1]
        for part in range(2):
            radial = squares[part] + across
            gain = 1.0 + radial * (1.0 / 0.05) + 0.25 * lax.rsqrt(radial + knee_sq)
            lanes = slice(128 * part, 128 * part + 128)
            gained[t, :, lanes] = gained[t, :, lanes] * (-gain)
        return carry

    lax.fori_loop(0, 16, gain_tile, 0)
    for q in range(2):
        tiles = slice(8 * q, 8 * q + 8)
        work[tiles] = mm_right(
            gained[tiles].reshape(512, 256), gent_h[...], gent_l[...]
        ).reshape(8, 64, 256)
    zero = mm_right(gained[:, 0:8, :].reshape(128, 256), spet_h[...], spet_l[...])
    work[:, 0:8, :] = jnp.where(special, zero.reshape(16, 8, 256), work[:, 0:8, :])
    for q in range(4):
        pieces = []
        for s in range(4):
            real, imag = work[4 * q + s, :, 0:128], work[4 * q + s, :, 128:256]
            pieces.append(
                jnp.concatenate(
                    [real * cos[...] - imag * sin[...], imag * cos[...] + real * sin[...]], axis=0
                )
            )
        both = jnp.concatenate(pieces, axis=1)
        out[:, 512 * q : 512 * q + 512] = mm_left(back_h[...], back_l[...], both)


def rows_back_kernel(data, cos, sin, gent_h, gent_l, spet_h, spet_l, out, work, done):
    for t in range(8):
        for c in range(2):
            block = data[:, 1024 * c + 128 * t : 1024 * c + 128 * t + 128]
            work[128 * t : 128 * t + 128, 128 * c : 128 * c + 128] = block.T
    for q in range(2):
        chunk = work[512 * q : 512 * q + 512]
        done[16 * q : 16 * q + 16] = mm_right(chunk, gent_h[...], gent_l[...]).reshape(16, 32, 256)
    done[0] = mm_right(work[0:32], spet_h[...], spet_l[...])

    def tile(i, carry):
        rows = aligned(i, 8)

        def load(k):
            return done[k, rows, 0:128], done[k, rows, 128:256]

        values = inverse_tile(load, cos, sin)
        for u in range(64):
            out[rows, 128 * u : 128 * u + 128] = values[u]
        return carry

    lax.fori_loop(0, 4, tile, 0)


def detect_kernel(
    slots, pointing, data, arrived, beam_t, cos, sin, gen_h, gen_l, spe_h, spe_l, weight, weight_zero,
    loading, spectrum, projected, points, picked, table, onehot, signal, work,
):
    for i in range(16):
        picked[32 * i : 32 * i + 32] = arrived[slots[i]]
    high, low = parts(mm_both(picked[...], beam_t[...]))
    table[:, 0:128] = high
    table[:, 128:256] = low
    points[:, 0:64] = pointing[...]
    points[:, 64:128] = pointing[...]
    lane = lax.broadcasted_iota(jnp.int32, (64, 512), 1)

    def gather(c, carry):
        turned = pltpu.roll(points[...], (128 - 8 * c) % 128, 1)
        for u in range(8):
            hit = turned[:, u : u + 1] == lane
            onehot[64 * u : 64 * u + 64] = jnp.where(hit, 1.0, 0.0).astype(BF16)
        both = mm(onehot[...], table[...])
        signal[aligned(c, 8)] = (both[:, 0:128] + both[:, 128:256]).reshape(8, 64, 128)
        return carry

    lax.fori_loop(0, 8, gather, 0)

    def tile(i, carry):
        rows = aligned(i, 8)
        values = [data[rows, 128 * u : 128 * u + 128] - signal[u, rows, :] for u in range(64)]

        def store(k, real, imag):
            work[k, rows, 0:128] = real
            work[k, rows, 128:256] = imag

        forward_tile(values, cos, sin, store)
        return carry

    lax.fori_loop(0, 8, tile, 0)

    def stage(q, carry):
        chunk = work[aligned(q, 8)].reshape(512, 256)
        spectrum[aligned(q, 8)] = mm_right(chunk, gen_h[...], gen_l[...]).reshape(8, 64, 256)
        return carry

    lax.fori_loop(0, 4, stage, 0)
    spectrum[0] = mm_right(work[0], spe_h[...], spe_l[...])
    left_h, left_l = parts(loading[...].T)

    def project(k, carry):
        first = jnp.where(k == 0, weight_zero[...], weight[...])
        scale = jnp.concatenate([first, weight[...]], axis=1)
        projected[k] = mm_left(left_h, left_l, spectrum[k] * scale)
        return carry

    lax.fori_loop(0, 32, project, 0)


def couple_kernel(place, shares, couple, couple_zero, out):
    def one(k, carry):
        total = shares[0, k]
        for s in range(1, shares.shape[0]):
            total = total + shares[s, k]
        pick = (place[0] == 0) & (k == 0)
        real = jnp.zeros((16, 128), F32)
        imag = jnp.zeros((16, 128), F32)
        for n in range(16):
            factor = couple[16 * n : 16 * n + 16]
            first = jnp.where(pick, couple_zero[16 * n : 16 * n + 16], factor)
            real = real + first * total[n : n + 1, 0:128]
            imag = imag + factor * total[n : n + 1, 128:256]
        out[k, :, 0:128] = real
        out[k, :, 128:256] = imag
        return carry

    lax.fori_loop(0, 4, one, 0)


def clean_kernel(
    slots, points, coupled, spectrum, weight, weight_zero, loading, beam, cos, sin, gent_h, gent_l,
    spet_h, spet_l, out, filtered, work, cleaned, onehot, total,
):
    left_h, left_l = parts(loading[...])

    def remove(k, carry):
        first = jnp.where(k == 0, weight_zero[...], weight[...])
        scale = jnp.concatenate([first, weight[...]], axis=1)
        filtered[k] = scale * (spectrum[k] - mm_left(left_h, left_l, coupled[k]))
        return carry

    lax.fori_loop(0, 32, remove, 0)

    def stage(q, carry):
        chunk = filtered[aligned(q, 8)].reshape(512, 256)
        work[aligned(q, 8)] = mm_right(chunk, gent_h[...], gent_l[...]).reshape(8, 64, 256)
        return carry

    lax.fori_loop(0, 4, stage, 0)
    work[0] = mm_right(filtered[0], spet_h[...], spet_l[...])

    def tile(i, carry):
        rows = aligned(i, 8)

        def load(k):
            return work[k, rows, 0:128], work[k, rows, 128:256]

        values = inverse_tile(load, cos, sin)
        for u in range(64):
            cleaned[u, rows, :] = values[u]
        return carry

    lax.fori_loop(0, 8, tile, 0)
    sub = lax.broadcasted_iota(jnp.int32, (512, 512), 0)
    total[...] = jnp.zeros((512, 256), F32)

    def scatter(c, carry):
        hit = points[pl.ds(c, 1), :] == sub
        onehot[...] = jnp.where(hit, 1.0, 0.0).astype(BF16)
        high, low = parts(cleaned[aligned(c, 8)].reshape(512, 128))
        total[...] += mm(onehot[...], jnp.concatenate([high, low], axis=1))
        return carry

    lax.fori_loop(0, 8, scatter, 0)
    summed = total[:, 0:128] + total[:, 128:256]
    grads = mm_both(summed, beam[...])
    out[...] = jnp.zeros((32, 32, 128), F32)
    for i in range(16):
        out[slots[i]] = grads[32 * i : 32 * i + 32]


def final_kernel(asked, delivered, prior, out):
    out[...] = prior[...]

    def step(i, carry):
        for c in range(2):
            block = asked[i, c]

            @pl.when(block < 64)
            def _():
                lanes = aligned(block, 128)
                out[:, lanes] = out[:, lanes] + delivered[2 * i + c]

        return carry

    lax.fori_loop(0, 16, step, 0)


SM = pltpu.SMEM


def call(kernel, ins, outs, scratch=(), out_spaces=None, spaces=None):
    spaces = spaces or {}
    in_specs = [pl.BlockSpec(memory_space=spaces.get(i, VM)) for i in range(len(ins))]
    out_spaces = out_spaces or [VM] * len(outs)
    out_specs = [pl.BlockSpec(memory_space=s) for s in out_spaces]
    shapes = [jax.ShapeDtypeStruct(s, d) for s, d in outs]
    result = pl.pallas_call(
        kernel,
        out_shape=shapes,
        in_specs=in_specs,
        out_specs=out_specs,
        scratch_shapes=list(scratch),
        compiler_params=pltpu.CompilerParams(vmem_limit_bytes=48 * 1024 * 1024),
        name=kernel.__name__,
    )(*ins)
    return result if len(outs) > 1 else result[0]


def row_constants():
    general, special = row_tables()
    cos, sin = twiddles(32, np.arange(128), 8192)
    scale = 2.0**-13
    return (
        (cos, sin),
        (*halves(general), *halves(special)),
        (*halves(general.T * scale), *halves(special.T * scale)),
    )


def col_constants():
    general, special = stage_tables(32, 4)
    left, back = real_left_table()
    cos, sin = twiddles(64, np.arange(128) % 32, 4096)
    return (
        (*halves(left), cos, sin),
        (*halves(general), *halves(special), *halves(general.T), *halves(special.T)),
        halves(back * 2.0**-12),
    )


def local(
    detector_data,
    sky_map,
    pointing,
    request_owner,
    request_block,
    beam_kernel,
    inv_white,
    mode_loading,
    mode_kernel,
):
    turn, ahead, behind = row_constants()
    start, middle, end = col_constants()
    band, band_zero = band_tables()
    det_rank = lax.axis_index("det")
    rank = (det_rank * lax.axis_size("tm") + lax.axis_index("tm")).astype(jnp.int32).reshape(1)

    send, slots = call(
        ids_kernel,
        (request_owner.reshape(16), request_block),
        [((16, 128), jnp.int32), ((16,), jnp.int32)],
        [SM((16,), jnp.int32)],
        [VM, SM],
        {0: SM, 1: SM},
    )
    asked = lax.all_to_all(send, "tm", split_axis=0, concat_axis=0, tiled=True)
    outgoing = call(pick_kernel, (asked, sky_map), [((32, 32, 128), F32)], spaces={0: SM})
    arrived = lax.all_to_all(outgoing, "tm", split_axis=0, concat_axis=0, tiled=True)

    packed = call(
        rows_kernel,
        (sky_map, *turn, *ahead),
        [((128, 2048), F32)],
        [VM((32, 32, 256), F32), VM((1024, 256), F32)],
    )
    columns = lax.all_to_all(packed, ("det", "tm"), split_axis=0, concat_axis=0, tiled=True)

    weight, weight_zero, couple, couple_zero = call(
        prep_kernel,
        (inv_white, band, band_zero, mode_kernel.transpose(2, 1, 0).reshape(256, NBAND)),
        [((64, 128), F32), ((64, 128), F32), ((256, 128), F32), ((256, 128), F32)],
    )
    spectrum, projected = call(
        detect_kernel,
        (
            slots, pointing, detector_data, arrived, beam_kernel.T, *turn, *ahead, weight, weight_zero,
            mode_loading,
        ),
        [((32, 64, 256), F32), ((32, 16, 256), F32)],
        [
            VM((64, 128), jnp.int32),
            VM((512, 128), F32),
            VM((512, 256), BF16),
            VM((512, 512), BF16),
            VM((64, 64, 128), F32),
            VM((32, 64, 256), F32),
        ],
        spaces={0: SM},
    )
    shares = lax.all_to_all(
        projected.reshape(8, 4, 16, 256), "det", split_axis=0, concat_axis=0, tiled=True
    )
    coupled = call(
        couple_kernel,
        (det_rank.astype(jnp.int32).reshape(1), shares, couple, couple_zero),
        [((4, 16, 256), F32)],
        spaces={0: SM},
    )
    coupled = lax.all_gather(coupled, "det", axis=0, tiled=True)

    filtered = call(
        columns_kernel,
        (rank, columns, *start, *middle, *end),
        [((128, 2048), F32)],
        [VM((16, 64, 256), F32), VM((16, 64, 256), F32)],
        spaces={0: SM},
    )
    returned_rows = lax.all_to_all(filtered, ("det", "tm"), split_axis=0, concat_axis=0, tiled=True)

    returned = call(
        clean_kernel,
        (
            slots, pointing.T.reshape(8, 512), coupled, spectrum, weight, weight_zero, mode_loading,
            beam_kernel, *turn, *behind,
        ),
        [((32, 32, 128), F32)],
        [
            VM((32, 64, 256), F32),
            VM((32, 64, 256), F32),
            VM((64, 64, 128), F32),
            VM((512, 512), BF16),
            VM((512, 256), F32),
        ],
        spaces={0: SM},
    )
    delivered = lax.all_to_all(returned, "tm", split_axis=0, concat_axis=0, tiled=True)
    prior = call(
        rows_back_kernel,
        (returned_rows, *turn, *behind),
        [((32, 8192), F32)],
        [VM((1024, 256), F32), VM((32, 32, 256), F32)],
    )
    return call(final_kernel, (asked, delivered, prior), [((32, 8192), F32)], spaces={0: SM})


def solution(mesh):
    return jax.shard_map(
        local,
        mesh=mesh,
        in_specs=(
            P("det", "tm"),
            P(("det", "tm"), None),
            P("det", "tm"),
            P(("det", "tm"), None),
            P(("det", "tm")),
            P(),
            P("det", None),
            P("det", None),
            P(),
        ),
        out_specs=P(("det", "tm"), None),
        check_vma=False,
    )
```

```python
import math

import jax
import jax.numpy as jnp
import numpy as np
from jax import lax
from jax.experimental import pallas as pl
from jax.experimental.pallas import tpu as pltpu
from jax.sharding import PartitionSpec as P


NBAND = 32
F32 = jnp.float32
BF16 = jnp.bfloat16
VM = pltpu.VMEM


def halves(table):
    high = np.asarray(table, np.float32).astype(BF16)
    low = (np.asarray(table, np.float64) - high.astype(np.float64)).astype(BF16)
    return high, low


def wave(rows, cols, period):
    turn = 2.0 * math.pi * ((rows[:, None] * cols[None, :]) % period) / period
    return np.cos(turn), np.sin(turn)


def stage_tables(width, copies):
    index = np.arange(width, dtype=np.float64)
    cos, sin = wave(index, index, width)
    half_cos, half_sin = wave(index, index + 0.5, width)
    eye = np.eye(copies)
    cos, sin = np.kron(eye, cos), np.kron(eye, sin)
    cas_half = np.kron(eye, half_cos + half_sin)
    zero = np.zeros_like(cos)
    general = np.block([[cos, -sin], [sin, cos]])
    special = np.block([[cos + sin, zero], [zero, cas_half]])
    return general, special


def row_tables():
    general, special = stage_tables(128, 1)
    return general, special


def twiddles(first, second, length):
    return [
        np.asarray(t, np.float32)
        for t in wave(np.arange(first, dtype=np.float64), second.astype(np.float64), length)
    ]


def real_left_table():
    index = np.arange(64, dtype=np.float64)
    cos, sin = wave(index, np.arange(128, dtype=np.float64), 128)
    forward = np.concatenate([cos, -sin], axis=0)
    forward[64] = np.cos(math.pi * np.arange(128))
    inverse = 2.0 * forward.T
    inverse[:, 0] = 1.0
    inverse[:, 64] = forward[64]
    return forward, inverse


def band_tables():
    second = np.arange(128)
    general = np.minimum(np.minimum(second, 127 - second) // 2, NBAND - 1)
    special = np.minimum(np.minimum(second, 128 - second) // 2, NBAND - 1)
    bands = np.arange(NBAND)[:, None]
    return (bands == general[None]).astype(np.float32), (bands == special[None]).astype(np.float32)


def turn_by(pair, quotient, count, sign):
    real, imag = pair
    cos = math.cos(2.0 * math.pi * quotient / count)
    sin = sign * math.sin(2.0 * math.pi * quotient / count)
    if 8 * quotient == count:
        scale = math.sqrt(0.5)
        if sign < 0:
            return (real + imag) * scale, (imag - real) * scale
        return (real - imag) * scale, (imag + real) * scale
    return real * cos - imag * sin, real * sin + imag * cos


def real_transform(values):
    count = len(values)
    if count == 1:
        return [(values[0], None)]
    if count == 2:
        return [(values[0] + values[1], None), (values[0] - values[1], None)]
    even = real_transform(values[0::2])
    odd = real_transform(values[1::2])
    half = count // 2
    out = [None] * (half + 1)
    out[0] = (even[0][0] + odd[0][0], None)
    out[half] = (even[0][0] - odd[0][0], None)
    for k in range(1, half // 2):
        turned = turn_by(odd[k], k, count, -1.0)
        out[k] = (even[k][0] + turned[0], even[k][1] + turned[1])
        out[half - k] = (even[k][0] - turned[0], turned[1] - even[k][1])
    out[half // 2] = (even[half // 2][0], -odd[half // 2][0])
    return out


def real_inverse(spectrum, count):
    if count == 1:
        return [spectrum[0][0]]
    first, last = spectrum[0][0], spectrum[count // 2][0]
    if count == 2:
        return [first + last, first - last]
    half = count // 2
    even = [None] * (half // 2 + 1)
    odd = [None] * (half // 2 + 1)
    even[0] = (first + last, None)
    odd[0] = (first - last, None)
    for k in range(1, half // 2):
        one, two = spectrum[k], spectrum[half - k]
        even[k] = (one[0] + two[0], one[1] - two[1])
        odd[k] = turn_by((one[0] - two[0], one[1] + two[1]), k, count, 1.0)
    middle = spectrum[half // 2]
    even[half // 2] = (middle[0] + middle[0], None)
    odd[half // 2] = (-(middle[1] + middle[1]), None)
    out = [None] * count
    out[0::2] = real_inverse(even, half)
    out[1::2] = real_inverse(odd, half)
    return out


def forward_tile(values, cos_ref, sin_ref, store):
    spectrum = real_transform(values)
    store(0, spectrum[0][0], spectrum[32][0])
    for k in range(1, 32):
        real, imag = spectrum[k]
        cos, sin = cos_ref[k : k + 1, :], sin_ref[k : k + 1, :]
        store(k, real * cos + imag * sin, imag * cos - real * sin)


def inverse_tile(load, cos_ref, sin_ref):
    first, last = load(0)
    spectrum = [(first, None)]
    for k in range(1, 32):
        real, imag = load(k)
        cos, sin = cos_ref[k : k + 1, :], sin_ref[k : k + 1, :]
        spectrum.append((real * cos - imag * sin, imag * cos + real * sin))
    spectrum.append((last, None))
    return real_inverse(spectrum, 64)


def parts(value):
    high = value.astype(BF16)
    return high, (value - high.astype(F32)).astype(BF16)


def mm(left, right):
    return jnp.dot(left, right, preferred_element_type=F32)


def mm_right(value, high, low):
    top, rest = parts(value)
    return mm(top, high) + mm(rest, high) + mm(top, low)


def mm_left(high, low, value):
    top, rest = parts(value)
    return mm(high, top) + mm(high, rest) + mm(low, top)


def mm_both(left, right):
    high, low = parts(right)
    return mm_right(left, high, low)


def aligned(index, size):
    return pl.ds(pl.multiple_of(index * size, size), size)


def ids_kernel(owner, block, send, slots, counts):
    for i in range(16):
        counts[i] = 0
    row = lax.broadcasted_iota(jnp.int32, (16, 128), 0)
    lane = lax.broadcasted_iota(jnp.int32, (16, 128), 1)
    table = jnp.full((16, 128), 64, jnp.int32)
    for i in range(16):
        target = owner[i]
        place = counts[target]
        counts[target] = place + 1
        slots[i] = target * 2 + place
        table = jnp.where((row == target) & (lane == place), block[i], table)
    send[...] = table


def pick_kernel(asked, sky, out, sem):
    copies = []
    for i in range(32):
        block = jnp.minimum(asked[i // 2, i % 2], 63)
        copies.append(pltpu.make_async_copy(sky.at[:, aligned(block, 128)], out.at[i], sem.at[i]))
        copies[-1].start()
    for copy in copies:
        copy.wait()


def exact(source, onehot):
    return jnp.dot(
        source, onehot, precision=lax.Precision.HIGHEST, preferred_element_type=F32
    )


def tables_kernel(kernel, bands, out):
    for part in range(2):
        out[part] = exact(kernel[...], bands[part])


def level_weights(inv_white, bands):
    levels = inv_white[...].T
    return exact(levels, bands[0]), exact(levels, bands[1])


def point_pairs(pointing, turned):
    wide = jnp.concatenate([pointing[...], pointing[...]], axis=0)
    turned[...] = jnp.concatenate([wide, wide], axis=1).T
    lane = lax.broadcasted_iota(jnp.int32, (32, 128), 1)
    even, odd = turned[pl.ds(0, 32, stride=2), :], turned[pl.ds(1, 32, stride=2), :]
    return jnp.where(lane < 64, even, odd)


def rows_kernel(sky, turn, later, out, work, done):
    def tile(i, carry):
        rows = aligned(i, 8)
        values = [sky[rows, 128 * u : 128 * u + 128] for u in range(64)]

        def store(k, real, imag):
            work[k, rows, 0:128] = real
            work[k, rows, 128:256] = imag

        forward_tile(values, turn[0], turn[1], store)
        return carry

    lax.fori_loop(0, 4, tile, 0)
    tables = later.wait()
    for q in range(2):
        chunk = work[16 * q : 16 * q + 16].reshape(512, 256)
        done[512 * q : 512 * q + 512] = mm_right(chunk, tables[0], tables[1])
    done[0:32] = mm_right(work[0], tables[2], tables[3])
    for t in range(8):
        for c in range(2):
            block = done[128 * t : 128 * t + 128, 128 * c : 128 * c + 128]
            out[pl.ds(8 * c + t, 128, stride=16), :] = block.T


def columns_kernel(
    meta, data, turn, ends, later, out, work, gained,
):
    cos, sin = turn.at[0], turn.at[1]
    for q in range(4):
        block = [data[pl.ds(4 * q + s, 128, stride=16), :] for s in range(4)]
        both = mm_left(ends[0], ends[1], jnp.concatenate(block, axis=1))
        for s in range(4):
            t = 4 * q + s
            real, imag = both[0:64, 128 * s : 128 * s + 128], both[64:128, 128 * s : 128 * s + 128]
            work[t, :, 0:128] = real * cos[...] + imag * sin[...]
            work[t, :, 128:256] = imag * cos[...] - real * sin[...]
    total_rows, total_cols = 4096, 8192
    row = lax.broadcasted_iota(jnp.int32, (64, 128), 0)
    lane = lax.broadcasted_iota(jnp.int32, (64, 128), 1)
    squares = []
    for part in range(2):
        vertical = row + 128 * (lane % 32)
        if part:
            vertical = jnp.where(row == 0, 64 + 128 * (lane % 32), vertical)
        folded = jnp.minimum(vertical, total_rows - vertical).astype(F32) / total_rows
        squares.append(folded * folded)
    lane8 = lax.broadcasted_iota(jnp.int32, (8, 128), 1)
    base = meta[1] * 64
    knee_sq = 1.0 / (2.0 * math.pi * (total_rows / 64.0)) ** 2
    special = lax.broadcasted_iota(jnp.int32, (16, 8, 256), 1) == 0
    tables = later.wait()
    for q in range(2):
        tiles = slice(8 * q, 8 * q + 8)
        gained[tiles] = mm_right(
            work[tiles].reshape(512, 256), tables[0], tables[1]
        ).reshape(8, 64, 256)
    zero = mm_right(work[:, 0:8, :].reshape(128, 256), tables[2], tables[3]).reshape(16, 8, 256)
    gained[:, 0:8, :] = jnp.where(special, zero, gained[:, 0:8, :])

    def gain_tile(t, carry):
        first = 4 * (t % 8) + lane8 // 32
        first = jnp.where((first == 0) & (t == 8), 32, first)
        horizontal = base + first
        folded = jnp.minimum(horizontal, total_cols - horizontal).astype(F32) / total_cols
        across = (folded * folded)[0:1]
        for part in range(2):
            radial = squares[part] + across
            gain = 1.0 + radial * (1.0 / 0.05) + 0.25 * lax.rsqrt(radial + knee_sq)
            lanes = slice(128 * part, 128 * part + 128)
            gained[t, :, lanes] = gained[t, :, lanes] * (-gain)
        return carry

    lax.fori_loop(0, 16, gain_tile, 0)
    for q in range(2):
        tiles = slice(8 * q, 8 * q + 8)
        work[tiles] = mm_right(
            gained[tiles].reshape(512, 256), tables[4], tables[5]
        ).reshape(8, 64, 256)
    zero = mm_right(gained[:, 0:8, :].reshape(128, 256), tables[6], tables[7])
    work[:, 0:8, :] = jnp.where(special, zero.reshape(16, 8, 256), work[:, 0:8, :])
    for q in range(4):
        pieces = []
        for s in range(4):
            real, imag = work[4 * q + s, :, 0:128], work[4 * q + s, :, 128:256]
            pieces.append(
                jnp.concatenate(
                    [real * cos[...] - imag * sin[...], imag * cos[...] + real * sin[...]], axis=0
                )
            )
        both = mm_left(ends[2], ends[3], jnp.concatenate(pieces, axis=1))
        for s in range(4):
            out[pl.ds(4 * q + s, 128, stride=16), :] = both[:, 128 * s : 128 * s + 128]


def rows_back_kernel(data, turn, later, out, work, done):
    for t in range(8):
        for c in range(2):
            block = data[pl.ds(8 * c + t, 128, stride=16), :]
            work[128 * t : 128 * t + 128, 128 * c : 128 * c + 128] = block.T
    tables = later.wait()
    for q in range(2):
        chunk = work[512 * q : 512 * q + 512]
        done[16 * q : 16 * q + 16] = mm_right(chunk, tables[0], tables[1]).reshape(16, 32, 256)
    done[0] = mm_right(work[0:32], tables[2], tables[3])

    def tile(i, carry):
        rows = aligned(i, 8)

        def load(k):
            return done[k, rows, 0:128], done[k, rows, 128:256]

        values = inverse_tile(load, turn[0], turn[1])
        for u in range(64):
            out[rows, 128 * u : 128 * u + 128] = values[u]
        return carry

    lax.fori_loop(0, 4, tile, 0)


def detect_kernel(
    meta, slots, pointing, data_later, arrived, beam, turn, tables_later, inv_white, bands, loading_t,
    spectrum_hbm, mine, theirs, points, picked, table, onehot, signal, work, spectrum, sem,
):
    weight, weight_zero = level_weights(inv_white, bands)
    for i in range(16):
        picked[32 * i : 32 * i + 32] = arrived[slots[i]]
    high, low = parts(mm_both(picked[...], beam[...].T))
    table[:, 0:128] = high
    table[:, 128:256] = low
    points[:, 0:64] = pointing[...]
    points[:, 64:128] = pointing[...]
    lane = lax.broadcasted_iota(jnp.int32, (64, 512), 1)

    def gather(c, carry):
        turned = pltpu.roll(points[...], (128 - 8 * c) % 128, 1)
        for u in range(8):
            hit = turned[:, u : u + 1] == lane
            onehot[64 * u : 64 * u + 64] = jnp.where(hit, 1.0, 0.0).astype(BF16)
        both = mm(onehot[...], table[...])
        signal[aligned(c, 8)] = (both[:, 0:128] + both[:, 128:256]).reshape(8, 64, 128)
        return carry

    lax.fori_loop(0, 8, gather, 0)
    data = data_later.wait()

    def tile(i, carry):
        rows = aligned(i, 8)
        values = [data[rows, 128 * u : 128 * u + 128] - signal[u, rows, :] for u in range(64)]

        def store(k, real, imag):
            work[k, rows, 0:128] = real
            work[k, rows, 128:256] = imag

        forward_tile(values, turn[0], turn[1], store)
        return carry

    lax.fori_loop(0, 8, tile, 0)

    tables = tables_later.wait()

    def stage(q, carry):
        chunk = work[aligned(q, 8)].reshape(512, 256)
        spectrum[aligned(q, 8)] = mm_right(chunk, tables[0], tables[1]).reshape(8, 64, 256)
        return carry

    lax.fori_loop(0, 4, stage, 0)
    spectrum[0] = mm_right(work[0], tables[2], tables[3])
    outward = pltpu.make_async_copy(spectrum, spectrum_hbm, sem)
    outward.start()
    left_h, left_l = parts(loading_t[...])
    core = meta[3]

    def project(i, carry):
        for out, side in ((theirs, 1 - core), (mine, core)):
            k = 8 * (i // 4) + 4 * side + i % 4
            first = jnp.where(k == 0, weight_zero, weight)
            scale = jnp.concatenate([first, weight], axis=1)
            out[i] = mm_left(left_h, left_l, spectrum[k] * scale)
        return carry

    lax.fori_loop(0, 16, project, 0, unroll=4)
    outward.wait()


def merge_kernel(meta, mine, theirs, *outs):
    for s in range(4):
        rows = aligned((meta[2] + s) % 4, 4)
        outs[s][...] = mine[rows] + theirs[rows]


def couple_kernel(meta, own, one, two, three, couple, out):
    for k in range(4):
        total = (own[k] + one[k]) + (two[k] + three[k])
        real = jnp.zeros((16, 128), F32)
        imag = jnp.zeros((16, 128), F32)
        for n in range(16):
            factor = couple[0, pl.ds(n, 16, stride=16), :]
            first = factor
            if k == 0:
                first = jnp.where(meta[0] == 0, couple[1, pl.ds(n, 16, stride=16), :], factor)
            real = real + first * total[n : n + 1, 0:128]
            imag = imag + factor * total[n : n + 1, 128:256]
        out[k, :, 0:128] = real
        out[k, :, 128:256] = imag


def clean_kernel(
    meta, slots, pointing, a0, a1, a2, a3, b0, b1, b2, b3, spectrum_hbm, inv_white, bands, loading_t,
    beam, turn, tables_later, out, filtered, work, cleaned, onehot, total, coupled, turned, points,
    spectrum, sem,
):
    inward = []
    for q in range(4):
        rows = slice(8 * q, 8 * q + 8)
        inward.append(pltpu.make_async_copy(spectrum_hbm.at[rows], spectrum.at[rows], sem.at[q]))
        inward[-1].start()
    for s, (here, there) in enumerate(((a0, b0), (a1, b1), (a2, b2), (a3, b3))):
        chip = (meta[2] + (4 - s)) % 4
        coupled[aligned(2 * chip + meta[3], 4)] = here[...]
        coupled[aligned(2 * chip + 1 - meta[3], 4)] = there[...]
    left_h, left_l = parts(loading_t[...].T)
    points[...] = point_pairs(pointing, turned)
    weight, weight_zero = level_weights(inv_white, bands)

    def remove(k, carry):
        first = jnp.where(k == 0, weight_zero, weight)
        scale = jnp.concatenate([first, weight], axis=1)
        filtered[k] = scale * (spectrum[k] - mm_left(left_h, left_l, coupled[k]))
        return carry

    for copy in inward:
        copy.wait()
    lax.fori_loop(0, 32, remove, 0, unroll=4)
    tables = tables_later.wait()

    def stage(q, carry):
        chunk = filtered[aligned(q, 8)].reshape(512, 256)
        work[aligned(q, 8)] = mm_right(chunk, tables[0], tables[1]).reshape(8, 64, 256)
        return carry

    lax.fori_loop(0, 4, stage, 0)
    work[0] = mm_right(filtered[0], tables[2], tables[3])

    def tile(i, carry):
        rows = aligned(i, 8)

        def load(k):
            return work[k, rows, 0:128], work[k, rows, 128:256]

        values = inverse_tile(load, turn[0], turn[1])
        for u in range(64):
            cleaned[u, rows, :] = values[u]
        return carry

    lax.fori_loop(0, 8, tile, 0)
    sub = lax.broadcasted_iota(jnp.int32, (512, 128), 0)
    total[...] = jnp.zeros((512, 256), F32)

    def scatter(c, carry):
        for u in range(4):
            hit = points[pl.ds(4 * c + u, 1), :] == sub
            onehot[:, 128 * u : 128 * u + 128] = jnp.where(hit, 1.0, 0.0).astype(BF16)
        high, low = parts(cleaned[aligned(c, 8)].reshape(512, 128))
        total[...] += mm(onehot[...], jnp.concatenate([high, low], axis=1))
        return carry

    lax.fori_loop(0, 8, scatter, 0)
    summed = total[:, 0:128] + total[:, 128:256]
    grads = mm_both(summed, beam[...])
    out[...] = jnp.zeros((32, 32, 128), F32)
    for i in range(16):
        out[slots[i]] = grads[32 * i : 32 * i + 32]


def final_kernel(asked, delivered, prior, out):
    out[...] = prior[...]

    def step(i, carry):
        for c in range(2):
            block = asked[i, c]

            @pl.when(block < 64)
            def _():
                lanes = aligned(block, 128)
                out[:, lanes] = out[:, lanes] + delivered[2 * i + c]

        return carry

    lax.fori_loop(0, 16, step, 0)


SM = pltpu.SMEM
HBM = pltpu.HBM
DMA = pltpu.SemaphoreType.DMA


class Later:
    def __init__(self, ref, copy):
        self.ref, self.copy = ref, copy

    def wait(self):
        self.copy.wait()
        return self.ref


def call(kernel, modes, ins, outs, scratch=(), out_spaces=None, limit=24):
    count, moved = len(ins), [i for i, m in enumerate(modes) if m in "etl"]
    spaces = {"v": VM, "s": SM}
    in_specs = [pl.BlockSpec(memory_space=spaces.get(m, HBM)) for m in modes]
    out_specs = [pl.BlockSpec(memory_space=s) for s in (out_spaces or [VM] * len(outs))]
    far = out_spaces or [VM] * len(outs)
    shapes = [
        HBM(s, d) if f is HBM else jax.ShapeDtypeStruct(s, d) for (s, d), f in zip(outs, far)
    ]
    buffers = [(SM if modes[i] == "t" else VM)(ins[i].shape, ins[i].dtype) for i in moved]

    def body(*refs):
        refs = list(refs)
        if moved:
            sems, targets = refs[-1], refs[-1 - len(moved) : -1]
            copies = []
            for n, (i, target) in enumerate(zip(moved, targets)):
                copies.append(pltpu.make_async_copy(refs[i], target, sems.at[n]))
                copies[-1].start()
            for i, target, copy in zip(moved, targets, copies):
                if modes[i] == "l":
                    refs[i] = Later(target, copy)
                else:
                    copy.wait()
                    refs[i] = target
            refs = refs[: -1 - len(moved)]
        kernel(*refs)

    run = pl.pallas_call(
        body,
        out_shape=shapes,
        in_specs=in_specs,
        out_specs=out_specs,
        scratch_shapes=list(scratch) + (buffers + [DMA((len(moved),))] if moved else []),
        compiler_params=pltpu.CompilerParams(vmem_limit_bytes=limit * 1024 * 1024),
    )
    assert len(modes) == count
    ins = [
        pltpu.with_memory_space_constraint(x, HBM) if m in "hetl" else x for x, m in zip(ins, modes)
    ]
    result = run(*ins)
    return result if len(outs) > 1 else result[0]


def row_constants():
    general, special = row_tables()
    turn = np.stack(twiddles(32, np.arange(128), 8192))
    scale = 2.0**-13
    ahead = np.stack([*halves(general), *halves(special)])
    behind = np.stack([*halves(general.T * scale), *halves(special.T * scale)])
    return turn, ahead, behind


def col_constants():
    general, special = stage_tables(32, 4)
    left, back = real_left_table()
    turn = np.stack(twiddles(64, np.arange(128) % 32, 4096))
    ends = np.stack([*halves(left), *halves(back * 2.0**-12)])
    tables = np.stack([*halves(general), *halves(special), *halves(general.T), *halves(special.T)])
    return turn, ends, tables


def exchange(value, axes):
    return lax.all_to_all(value, axes, split_axis=0, concat_axis=0, tiled=True)


def core_swap(value):
    return lax.ppermute(value, "det", [(g, g ^ 1) for g in range(8)])


def chip_shift(value, step):
    return lax.ppermute(value, "det", [(g, (g + 2 * step) % 8) for g in range(8)])


def local(
    detector_data,
    sky_map,
    pointing,
    request_owner,
    request_block,
    beam_kernel,
    inv_white,
    mode_loading,
    mode_kernel,
):
    turn, ahead, behind = (jnp.asarray(t) for t in row_constants())
    col_turn, ends, tables = (jnp.asarray(t) for t in col_constants())
    bands = jnp.asarray(np.stack(band_tables()))
    det = lax.axis_index("det").astype(jnp.int32)
    rank = det * lax.axis_size("tm") + lax.axis_index("tm").astype(jnp.int32)
    meta = jnp.stack([det, rank, det // 2, det % 2])
    square, half = VM((32, 64, 256), F32), VM((32, 32, 256), F32)
    flat = (32, 32, 128)
    loading_t, inv_white = mode_loading.T, inv_white.T

    send, slots = call(
        ids_kernel,
        "tt",
        (request_owner.reshape(16), request_block),
        [((16, 128), jnp.int32), ((16,), jnp.int32)],
        [SM((16,), jnp.int32)],
        [VM, SM],
    )
    asked = exchange(send, "tm")
    outgoing = call(pick_kernel, "sh", (asked, sky_map), [(flat, F32)], [DMA((32,))])
    arrived = exchange(outgoing, "tm")

    wide = ((2048, 128), F32)
    packed = call(
        rows_kernel, "eel", (sky_map, turn, ahead), [wide], [half, VM((1024, 256), F32)]
    )
    columns = exchange(packed.reshape(128, 16, 128), ("det", "tm"))

    spectrum, mine, theirs = call(
        detect_kernel,
        "sselveeleee",
        (
            meta, slots, pointing, detector_data, arrived, beam_kernel, turn, ahead, inv_white, bands,
            loading_t,
        ),
        [((32, 64, 256), F32), ((16, 16, 256), F32), ((16, 16, 256), F32)],
        [
            VM((64, 128), jnp.int32),
            VM((512, 128), F32),
            VM((512, 256), BF16),
            VM((512, 512), BF16),
            VM((64, 64, 128), F32),
            square,
            square,
            DMA,
        ],
        [HBM, VM, VM],
    )
    share = ((4, 16, 256), F32)
    partner = core_swap(theirs)
    sums = call(merge_kernel, "svv", (meta, mine, partner), [share] * 4)
    couple = call(
        tables_kernel,
        "ee",
        (mode_kernel.transpose(1, 2, 0).reshape(256, NBAND), bands),
        [((2, 256, 128), F32)],
    )
    gathered = [sums[0]] + [chip_shift(sums[s], s) for s in range(1, 4)]
    coupled = call(couple_kernel, "svvvvv", (meta, *gathered, couple), [share])
    here = [coupled] + [chip_shift(coupled, s) for s in range(1, 4)]
    there = [core_swap(coupled)]
    there += [core_swap(value) for value in here[1:]]

    filtered = call(
        columns_kernel,
        "sveel",
        (meta, columns.reshape(2048, 128), col_turn, ends, tables),
        [wide],
        [VM((16, 64, 256), F32), VM((16, 64, 256), F32)],
    )
    returned_rows = exchange(filtered.reshape(128, 16, 128), ("det", "tm"))

    returned = call(
        clean_kernel,
        "sse" + "v" * 8 + "heeeeel",
        (
            meta, slots, pointing, *here, *there, spectrum, inv_white, bands, loading_t, beam_kernel,
            turn, behind,
        ),
        [(flat, F32)],
        [
            square,
            square,
            VM((64, 64, 128), F32),
            VM((512, 512), BF16),
            VM((512, 256), F32),
            VM((32, 16, 256), F32),
            VM((128, 128), jnp.int32),
            VM((32, 128), jnp.int32),
            square,
            DMA((4,)),
        ],
    )
    delivered = exchange(returned, "tm")
    prior = call(
        rows_back_kernel,
        "vel",
        (returned_rows.reshape(2048, 128), turn, behind),
        [((32, 8192), F32)],
        [VM((1024, 256), F32), half],
    )
    return call(final_kernel, "svv", (asked, delivered, prior), [((32, 8192), F32)])


def solution(mesh):
    return jax.shard_map(
        local,
        mesh=mesh,
        in_specs=(
            P("det", "tm"),
            P(("det", "tm"), None),
            P("det", "tm"),
            P(("det", "tm"), None),
            P(("det", "tm")),
            P(),
            P("det", None),
            P("det", None),
            P(),
        ),
        out_specs=P(("det", "tm"), None),
        check_vma=False,
    )
```

```python
import math

import jax
import jax.numpy as jnp
import numpy as np
from jax import lax
from jax.experimental import pallas as pl
from jax.experimental.pallas import tpu as pltpu
from jax.sharding import PartitionSpec as P


NBAND = 32
F32 = jnp.float32
BF16 = jnp.bfloat16
VM = pltpu.VMEM


def halves(table):
    high = np.asarray(table, np.float32).astype(BF16)
    low = (np.asarray(table, np.float64) - high.astype(np.float64)).astype(BF16)
    return high, low


def wave(rows, cols, period):
    turn = 2.0 * math.pi * ((rows[:, None] * cols[None, :]) % period) / period
    return np.cos(turn), np.sin(turn)


def stage_tables(width, copies):
    index = np.arange(width, dtype=np.float64)
    cos, sin = wave(index, index, width)
    half_cos, half_sin = wave(index, index + 0.5, width)
    eye = np.eye(copies)
    cos, sin = np.kron(eye, cos), np.kron(eye, sin)
    cas_half = np.kron(eye, half_cos + half_sin)
    zero = np.zeros_like(cos)
    general = np.block([[cos, -sin], [sin, cos]])
    special = np.block([[cos + sin, zero], [zero, cas_half]])
    return general, special


def row_tables():
    general, special = stage_tables(128, 1)
    return general, special


def twiddles(first, second, length):
    return [
        np.asarray(t, np.float32)
        for t in wave(np.arange(first, dtype=np.float64), second.astype(np.float64), length)
    ]


def band_tables():
    second = np.arange(128)
    general = np.minimum(np.minimum(second, 127 - second) // 2, NBAND - 1)
    special = np.minimum(np.minimum(second, 128 - second) // 2, NBAND - 1)
    bands = np.arange(NBAND)[:, None]
    return (bands == general[None]).astype(np.float32), (bands == special[None]).astype(np.float32)


def turn_by(pair, quotient, count, sign):
    real, imag = pair
    cos = math.cos(2.0 * math.pi * quotient / count)
    sin = sign * math.sin(2.0 * math.pi * quotient / count)
    if 8 * quotient == count:
        scale = math.sqrt(0.5)
        if sign < 0:
            return (real + imag) * scale, (imag - real) * scale
        return (real - imag) * scale, (imag + real) * scale
    return real * cos - imag * sin, real * sin + imag * cos


def real_transform(values):
    count = len(values)
    if count == 1:
        return [(values[0], None)]
    if count == 2:
        return [(values[0] + values[1], None), (values[0] - values[1], None)]
    even = real_transform(values[0::2])
    odd = real_transform(values[1::2])
    half = count // 2
    out = [None] * (half + 1)
    out[0] = (even[0][0] + odd[0][0], None)
    out[half] = (even[0][0] - odd[0][0], None)
    for k in range(1, half // 2):
        turned = turn_by(odd[k], k, count, -1.0)
        out[k] = (even[k][0] + turned[0], even[k][1] + turned[1])
        out[half - k] = (even[k][0] - turned[0], turned[1] - even[k][1])
    out[half // 2] = (even[half // 2][0], -odd[half // 2][0])
    return out


def real_inverse(spectrum, count):
    if count == 1:
        return [spectrum[0][0]]
    first, last = spectrum[0][0], spectrum[count // 2][0]
    if count == 2:
        return [first + last, first - last]
    half = count // 2
    even = [None] * (half // 2 + 1)
    odd = [None] * (half // 2 + 1)
    even[0] = (first + last, None)
    odd[0] = (first - last, None)
    for k in range(1, half // 2):
        one, two = spectrum[k], spectrum[half - k]
        even[k] = (one[0] + two[0], one[1] - two[1])
        odd[k] = turn_by((one[0] - two[0], one[1] + two[1]), k, count, 1.0)
    middle = spectrum[half // 2]
    even[half // 2] = (middle[0] + middle[0], None)
    odd[half // 2] = (-(middle[1] + middle[1]), None)
    out = [None] * count
    out[0::2] = real_inverse(even, half)
    out[1::2] = real_inverse(odd, half)
    return out


def forward_tile(values, cos_ref, sin_ref, store):
    half = len(values) // 2
    spectrum = real_transform(values)
    store(0, spectrum[0][0], spectrum[half][0])
    for k in range(1, half):
        real, imag = spectrum[k]
        cos, sin = cos_ref[k : k + 1, :], sin_ref[k : k + 1, :]
        store(k, real * cos + imag * sin, imag * cos - real * sin)


def inverse_tile(load, cos_ref, sin_ref, half=32):
    first, last = load(0)
    spectrum = [(first, None)]
    for k in range(1, half):
        real, imag = load(k)
        cos, sin = cos_ref[k : k + 1, :], sin_ref[k : k + 1, :]
        spectrum.append((real * cos - imag * sin, imag * cos + real * sin))
    spectrum.append((last, None))
    return real_inverse(spectrum, 2 * half)


def parts(value):
    high = value.astype(BF16)
    return high, (value - high.astype(F32)).astype(BF16)


def mm(left, right):
    return jnp.dot(left, right, preferred_element_type=F32)


def mm_right(value, high, low):
    top, rest = parts(value)
    return mm(top, high) + mm(rest, high) + mm(top, low)


def mm_left(high, low, value):
    top, rest = parts(value)
    return mm(high, top) + mm(high, rest) + mm(low, top)


def mm_both(left, right):
    high, low = parts(right)
    return mm_right(left, high, low)


def aligned(index, size):
    return pl.ds(pl.multiple_of(index * size, size), size)


def ids_kernel(owner, block, send, slots, counts):
    for i in range(16):
        counts[i] = 0
    row = lax.broadcasted_iota(jnp.int32, (16, 128), 0)
    lane = lax.broadcasted_iota(jnp.int32, (16, 128), 1)
    table = jnp.full((16, 128), 64, jnp.int32)
    for i in range(16):
        target = owner[i]
        place = counts[target]
        counts[target] = place + 1
        slots[i] = target * 2 + place
        table = jnp.where((row == target) & (lane == place), block[i], table)
    send[...] = table


def pick_kernel(asked, sky, out, sem):
    copies = []
    for i in range(32):
        block = jnp.minimum(asked[i // 2, i % 2], 63)
        copies.append(pltpu.make_async_copy(sky.at[:, aligned(block, 128)], out.at[i], sem.at[i]))
        copies[-1].start()
    for copy in copies:
        copy.wait()


def exact(source, onehot):
    return jnp.dot(
        source, onehot, precision=lax.Precision.HIGHEST, preferred_element_type=F32
    )


def level_weights(inv_white, bands):
    levels = inv_white[...].T
    return exact(levels, bands[0]), exact(levels, bands[1])


def point_pairs(pointing, turned):
    wide = jnp.concatenate([pointing[...], pointing[...]], axis=0)
    turned[...] = jnp.concatenate([wide, wide], axis=1).T
    lane = lax.broadcasted_iota(jnp.int32, (32, 128), 1)
    even, odd = turned[pl.ds(0, 32, stride=2), :], turned[pl.ds(1, 32, stride=2), :]
    return jnp.where(lane < 64, even, odd)


def rows_kernel(sky, turn, later, out, work, done):
    def tile(i, carry):
        rows = aligned(i, 8)
        values = [sky[rows, 128 * u : 128 * u + 128] for u in range(64)]

        def store(k, real, imag):
            work[k, rows, 0:128] = real
            work[k, rows, 128:256] = imag

        forward_tile(values, turn[0], turn[1], store)
        return carry

    lax.fori_loop(0, 4, tile, 0)
    tables = later.wait()
    for q in range(2):
        chunk = work[16 * q : 16 * q + 16].reshape(512, 256)
        done[512 * q : 512 * q + 512] = mm_right(chunk, tables[0], tables[1])
    done[0:32] = mm_right(work[0], tables[2], tables[3])
    for t in range(8):
        for c in range(2):
            block = done[128 * t : 128 * t + 128, 128 * c : 128 * c + 128]
            out[pl.ds(8 * c + t, 128, stride=16), :] = block.T


def columns_kernel(meta, data, turn, tables, out_hbm, work, gained, out, sems):
    def ahead(i, carry):
        tiles = aligned(i, 8)

        def store(k, real, imag):
            work[k, tiles, 0:128] = real
            work[k, tiles, 128:256] = imag

        forward_tile([data[d, tiles, :] for d in range(128)], turn[0], turn[1], store)
        return carry

    lax.fori_loop(0, 2, ahead, 0)
    total_rows, total_cols = 4096, 8192
    tile = lax.broadcasted_iota(jnp.int32, (16, 128), 0)
    lane = lax.broadcasted_iota(jnp.int32, (16, 128), 1)
    first = 4 * (tile % 8) + lane // 32
    first = jnp.where((first == 0) & (tile == 8), 32, first)
    horizontal = meta[1] * 64 + first
    lane_row = lax.broadcasted_iota(jnp.int32, (1, 128), 1)
    folded = jnp.minimum(horizontal, total_cols - horizontal).astype(F32) / total_cols
    across = folded * folded
    knee_sq = 1.0 / (2.0 * math.pi * (total_rows / 64.0)) ** 2

    def middle(q, carry):
        chunk = work[aligned(q, 16)].reshape(256, 256)
        gained[aligned(q, 16)] = mm_right(chunk, tables[0], tables[1]).reshape(16, 16, 256)

        @pl.when(q == 0)
        def _():
            gained[0] = mm_right(work[0], tables[2], tables[3])

        for j in range(16):
            k = 16 * q + j
            for part in range(2):
                lead = jnp.where((k == 0) & (part == 1), 64, k)
                vertical = lead + 128 * (lane_row % 32)
                fold = jnp.minimum(vertical, total_rows - vertical).astype(F32) / total_rows
                radial = fold * fold + across
                gain = 1.0 + radial * (1.0 / 0.05) + 0.25 * lax.rsqrt(radial + knee_sq)
                lanes = slice(128 * part, 128 * part + 128)
                gained[k, :, lanes] = gained[k, :, lanes] * (-gain)
        chunk = gained[aligned(q, 16)].reshape(256, 256)
        work[aligned(q, 16)] = mm_right(chunk, tables[4], tables[5]).reshape(16, 16, 256)

        @pl.when(q == 0)
        def _():
            work[0] = mm_right(gained[0], tables[6], tables[7])

        return carry

    lax.fori_loop(0, 4, middle, 0)

    def outward(i):
        return pltpu.make_async_copy(out.at[i], out_hbm.at[:, aligned(i, 8)], sems.at[i])

    def behind(i, carry):
        tiles = aligned(i, 8)

        def load(k):
            return work[k, tiles, 0:128], work[k, tiles, 128:256]

        values = inverse_tile(load, turn[0], turn[1], 64)
        for d in range(128):
            out[i, d] = values[d]
        outward(i).start()
        return carry

    lax.fori_loop(0, 2, behind, 0)
    for i in range(2):
        outward(i).wait()


def rows_back_kernel(data, turn, later, out, work, done):
    for t in range(8):
        for c in range(2):
            block = data[pl.ds(8 * c + t, 128, stride=16), :]
            work[128 * t : 128 * t + 128, 128 * c : 128 * c + 128] = block.T
    tables = later.wait()
    for q in range(2):
        chunk = work[512 * q : 512 * q + 512]
        done[16 * q : 16 * q + 16] = mm_right(chunk, tables[0], tables[1]).reshape(16, 32, 256)
    done[0] = mm_right(work[0:32], tables[2], tables[3])

    def tile(i, carry):
        rows = aligned(i, 8)

        def load(k):
            return done[k, rows, 0:128], done[k, rows, 128:256]

        values = inverse_tile(load, turn[0], turn[1])
        for u in range(64):
            out[rows, 128 * u : 128 * u + 128] = values[u]
        return carry

    lax.fori_loop(0, 4, tile, 0)


def stage_kernel(
    inv_white, bands, loading_t, kernel, pointing, *refs
):
    sources, targets = refs[:5], refs[5:10]
    weights, couple, mixing, pairs, turned, sems = refs[10:]
    copies = [pltpu.make_async_copy(a, b, sems.at[n]) for n, (a, b) in enumerate(zip(sources, targets))]
    for copy in copies:
        copy.start()
    weights[0], weights[1] = level_weights(inv_white, bands)
    for part in range(2):
        couple[part] = exact(kernel[...], bands[part])
    mixing[...] = loading_t[...].T
    pairs[...] = point_pairs(pointing, turned)
    for copy in copies:
        copy.wait()


def detect_kernel(
    meta, slots, pointing, data_later, arrived, beam, turn, tables, weights, loading_t, spectrum_hbm, mine,
    theirs, points, picked, table, onehot, signal, work, spectrum, sems,
):
    weight, weight_zero = weights[0], weights[1]
    for i in range(16):
        picked[32 * i : 32 * i + 32] = arrived[slots[i]]
    high, low = parts(mm_both(picked[...], beam[...].T))
    table[:, 0:128] = high
    table[:, 128:256] = low
    points[:, 0:64] = pointing[...]
    points[:, 64:128] = pointing[...]
    lane = lax.broadcasted_iota(jnp.int32, (64, 512), 1)

    def gather(c, carry):
        moved = pltpu.roll(points[...], (128 - 8 * c) % 128, 1)
        for u in range(8):
            hit = moved[:, u : u + 1] == lane
            onehot[64 * u : 64 * u + 64] = jnp.where(hit, 1.0, 0.0).astype(BF16)
        both = mm(onehot[...], table[...])
        signal[aligned(c, 8)] = (both[:, 0:128] + both[:, 128:256]).reshape(8, 64, 128)
        return carry

    lax.fori_loop(0, 8, gather, 0)
    data = data_later.wait()

    def tile(i, carry):
        rows = aligned(i, 8)
        values = [data[rows, 128 * u : 128 * u + 128] - signal[u, rows, :] for u in range(64)]

        def store(k, real, imag):
            work[k, rows, 0:128] = real
            work[k, rows, 128:256] = imag

        forward_tile(values, turn[0], turn[1], store)
        return carry

    lax.fori_loop(0, 8, tile, 0)

    def outward(q):
        rows = aligned(q, 8)
        return pltpu.make_async_copy(spectrum.at[rows], spectrum_hbm.at[rows], sems.at[q])

    def stage(q, carry):
        chunk = work[aligned(q, 8)].reshape(512, 256)
        spectrum[aligned(q, 8)] = mm_right(chunk, tables[0], tables[1]).reshape(8, 64, 256)

        @pl.when(q == 0)
        def _():
            spectrum[0] = mm_right(work[0], tables[2], tables[3])

        outward(q).start()
        return carry

    lax.fori_loop(0, 4, stage, 0)
    left_h, left_l = parts(loading_t[...])
    core = meta[3]

    def project(i, carry):
        for out, side in ((theirs, 1 - core), (mine, core)):
            k = 8 * (i // 4) + 4 * side + i % 4
            first = jnp.where(k == 0, weight_zero, weight)
            scale = jnp.concatenate([first, weight], axis=1)
            out[i] = mm_left(left_h, left_l, spectrum[k] * scale)
        return carry

    lax.fori_loop(0, 16, project, 0, unroll=4)
    for q in range(4):
        outward(q).wait()


def merge_kernel(meta, mine, theirs, *outs):
    for s in range(4):
        rows = aligned((meta[2] + s) % 4, 4)
        outs[s][...] = mine[rows] + theirs[rows]


def couple_kernel(meta, own, one, two, three, couple, out):
    for k in range(4):
        total = (own[k] + one[k]) + (two[k] + three[k])
        real = jnp.zeros((16, 128), F32)
        imag = jnp.zeros((16, 128), F32)
        for n in range(16):
            factor = couple[0, pl.ds(n, 16, stride=16), :]
            first = factor
            if k == 0:
                first = jnp.where(meta[0] == 0, couple[1, pl.ds(n, 16, stride=16), :], factor)
            real = real + first * total[n : n + 1, 0:128]
            imag = imag + factor * total[n : n + 1, 128:256]
        out[k, :, 0:128] = real
        out[k, :, 128:256] = imag


def clean_kernel(
    meta, slots, pairs, a0, a1, a2, a3, b0, b1, b2, b3, spectrum_later, weights, mixing, beam, turn,
    tables_later, out, filtered, work, cleaned, onehot, total, coupled,
):
    for s, (here, there) in enumerate(((a0, b0), (a1, b1), (a2, b2), (a3, b3))):
        chip = (meta[2] + (4 - s)) % 4
        coupled[aligned(2 * chip + meta[3], 4)] = here[...]
        coupled[aligned(2 * chip + 1 - meta[3], 4)] = there[...]
    left_h, left_l = parts(mixing[...])
    weight, weight_zero = weights[0], weights[1]

    def remove(k, carry):
        first = jnp.where(k == 0, weight_zero, weight)
        scale = jnp.concatenate([first, weight], axis=1)
        filtered[k] = scale * (spectrum[k] - mm_left(left_h, left_l, coupled[k]))
        return carry

    spectrum = spectrum_later.wait()
    lax.fori_loop(0, 32, remove, 0, unroll=4)
    tables = tables_later.wait()

    def stage(q, carry):
        chunk = filtered[aligned(q, 8)].reshape(512, 256)
        work[aligned(q, 8)] = mm_right(chunk, tables[0], tables[1]).reshape(8, 64, 256)
        return carry

    lax.fori_loop(0, 4, stage, 0)
    work[0] = mm_right(filtered[0], tables[2], tables[3])

    def tile(i, carry):
        rows = aligned(i, 8)

        def load(k):
            return work[k, rows, 0:128], work[k, rows, 128:256]

        values = inverse_tile(load, turn[0], turn[1])
        for u in range(64):
            cleaned[u, rows, :] = values[u]
        return carry

    lax.fori_loop(0, 8, tile, 0)
    sub = lax.broadcasted_iota(jnp.int32, (512, 128), 0)
    total[...] = jnp.zeros((512, 256), F32)

    def scatter(c, carry):
        for u in range(4):
            hit = pairs[pl.ds(4 * c + u, 1), :] == sub
            onehot[:, 128 * u : 128 * u + 128] = jnp.where(hit, 1.0, 0.0).astype(BF16)
        high, low = parts(cleaned[aligned(c, 8)].reshape(512, 128))
        total[...] += mm(onehot[...], jnp.concatenate([high, low], axis=1))
        return carry

    lax.fori_loop(0, 8, scatter, 0)
    summed = total[:, 0:128] + total[:, 128:256]
    grads = mm_both(summed, beam[...])
    out[...] = jnp.zeros((32, 32, 128), F32)
    for i in range(16):
        out[slots[i]] = grads[32 * i : 32 * i + 32]


def final_kernel(asked, delivered, prior, out):
    out[...] = prior[...]

    def step(i, carry):
        for c in range(2):
            block = asked[i, c]

            @pl.when(block < 64)
            def _():
                lanes = aligned(block, 128)
                out[:, lanes] = out[:, lanes] + delivered[2 * i + c]

        return carry

    lax.fori_loop(0, 16, step, 0)


SM = pltpu.SMEM
HBM = pltpu.HBM
DMA = pltpu.SemaphoreType.DMA
KEEP = "keep"


class Later:
    def __init__(self, ref, copy):
        self.ref, self.copy = ref, copy

    def wait(self):
        self.copy.wait()
        return self.ref


def call(kernel, modes, ins, outs, scratch=(), out_spaces=None, limit=24):
    count, moved = len(ins), [i for i, m in enumerate(modes) if m in "etl"]
    spaces = {"v": VM, "w": VM, "s": SM}
    in_specs = [pl.BlockSpec(memory_space=spaces.get(m, HBM)) for m in modes]
    out_specs = [
        pl.BlockSpec(memory_space=VM if s is KEEP else s) for s in (out_spaces or [VM] * len(outs))
    ]
    far = out_spaces or [VM] * len(outs)
    shapes = [
        (VM if f is KEEP else HBM)(s, d) if f in (HBM, KEEP) else jax.ShapeDtypeStruct(s, d)
        for (s, d), f in zip(outs, far)
    ]
    buffers = [(SM if modes[i] == "t" else VM)(ins[i].shape, ins[i].dtype) for i in moved]

    def body(*refs):
        refs = list(refs)
        if moved:
            sems, targets = refs[-1], refs[-1 - len(moved) : -1]
            copies = []
            for n, (i, target) in enumerate(zip(moved, targets)):
                copies.append(pltpu.make_async_copy(refs[i], target, sems.at[n]))
            for kind in ("et", "l"):
                for i, copy in zip(moved, copies):
                    if modes[i] in kind:
                        copy.start()
            for i, target, copy in zip(moved, targets, copies):
                if modes[i] == "l":
                    refs[i] = Later(target, copy)
                else:
                    copy.wait()
                    refs[i] = target
            refs = refs[: -1 - len(moved)]
        kernel(*refs)

    run = pl.pallas_call(
        body,
        out_shape=shapes,
        in_specs=in_specs,
        out_specs=out_specs,
        scratch_shapes=list(scratch) + (buffers + [DMA((len(moved),))] if moved else []),
        compiler_params=pltpu.CompilerParams(vmem_limit_bytes=limit * 1024 * 1024),
    )
    assert len(modes) == count
    ins = [
        pltpu.with_memory_space_constraint(x, VM if m == "w" else HBM) if m in "hetlw" else x
        for x, m in zip(ins, modes)
    ]
    result = run(*ins)
    return result if len(outs) > 1 else result[0]


def row_constants():
    general, special = row_tables()
    turn = np.stack(twiddles(32, np.arange(128), 8192))
    scale = 2.0**-13
    ahead = np.stack([*halves(general), *halves(special)])
    behind = np.stack([*halves(general.T * scale), *halves(special.T * scale)])
    return turn, ahead, behind


def col_constants():
    general, special = stage_tables(32, 4)
    turn = np.stack(twiddles(64, np.arange(128) % 32, 4096))
    scale = 2.0**-12
    behind = (*halves(general.T * scale), *halves(special.T * scale))
    return turn, np.stack([*halves(general), *halves(special), *behind])


def exchange(value, axes):
    return lax.all_to_all(value, axes, split_axis=0, concat_axis=0, tiled=True)


def core_swap(value):
    return lax.ppermute(value, "det", [(g, g ^ 1) for g in range(8)])


def chip_shift(value, step):
    return lax.ppermute(value, "det", [(g, (g + 2 * step) % 8) for g in range(8)])


def local(
    detector_data,
    sky_map,
    pointing,
    request_owner,
    request_block,
    beam_kernel,
    inv_white,
    mode_loading,
    mode_kernel,
):
    turn, ahead, behind = (jnp.asarray(t) for t in row_constants())
    col_turn, tables = (jnp.asarray(t) for t in col_constants())
    bands = jnp.asarray(np.stack(band_tables()))
    det = lax.axis_index("det").astype(jnp.int32)
    rank = det * lax.axis_size("tm") + lax.axis_index("tm").astype(jnp.int32)
    meta = jnp.stack([det, rank, det // 2, det % 2])
    square, half = VM((32, 64, 256), F32), VM((32, 32, 256), F32)
    flat = (32, 32, 128)
    loading_t, inv_white = mode_loading.T, inv_white.T

    send, slots = call(
        ids_kernel,
        "tt",
        (request_owner.reshape(16), request_block),
        [((16, 128), jnp.int32), ((16,), jnp.int32)],
        [SM((16,), jnp.int32)],
        [VM, SM],
    )
    asked = exchange(send, "tm")
    outgoing = call(pick_kernel, "sh", (asked, sky_map), [(flat, F32)], [DMA((32,))])
    arrived = exchange(outgoing, "tm")

    wide = ((2048, 128), F32)
    packed = call(
        rows_kernel, "eel", (sky_map, turn, ahead), [wide], [half, VM((1024, 256), F32)]
    )
    columns = exchange(packed.reshape(128, 16, 128), ("det", "tm"))

    moved = (turn, ahead, beam_kernel, col_turn, tables)
    turn_v, ahead_v, beam_v, col_turn_v, tables_v, weights, couple, mixing, pairs = call(
        stage_kernel,
        "eeeeehhhhh",
        (
            inv_white, bands, loading_t, mode_kernel.transpose(1, 2, 0).reshape(256, NBAND), pointing,
            *moved,
        ),
        [(m.shape, m.dtype) for m in moved]
        + [
            ((2, 64, 128), F32),
            ((2, 256, 128), F32),
            ((64, 16), F32),
            ((32, 128), jnp.int32),
        ],
        [VM((128, 128), jnp.int32), DMA((5,))],
        [KEEP] * 9,
    )
    spectrum, mine, theirs = call(
        detect_kernel,
        "sselvwwwwe",
        (meta, slots, pointing, detector_data, arrived, beam_v, turn_v, ahead_v, weights, loading_t),
        [((32, 64, 256), F32), ((16, 16, 256), F32), ((16, 16, 256), F32)],
        [
            VM((64, 128), jnp.int32),
            VM((512, 128), F32),
            VM((512, 256), BF16),
            VM((512, 512), BF16),
            VM((64, 64, 128), F32),
            square,
            square,
            DMA((4,)),
        ],
        [HBM, VM, VM],
    )
    share = ((4, 16, 256), F32)
    partner = core_swap(theirs)
    sums = call(merge_kernel, "svv", (meta, mine, partner), [share] * 4)
    gathered = [sums[0]] + [chip_shift(sums[s], s) for s in range(1, 4)]
    coupled = call(couple_kernel, "svvvvw", (meta, *gathered, couple), [share])
    here = [coupled] + [chip_shift(coupled, s) for s in range(1, 4)]
    there = [core_swap(value) for value in here]

    filtered = call(
        columns_kernel,
        "svww",
        (meta, columns, col_turn_v, tables_v),
        [((128, 16, 128), F32)],
        [VM((64, 16, 256), F32), VM((64, 16, 256), F32), VM((2, 128, 8, 128), F32), DMA((2,))],
        [HBM],
    )
    returned_rows = exchange(filtered, ("det", "tm"))

    returned = call(
        clean_kernel,
        "ssw" + "v" * 8 + "lwwwwl",
        (meta, slots, pairs, *here, *there, spectrum, weights, mixing, beam_v, turn_v, behind),
        [(flat, F32)],
        [
            square,
            square,
            VM((64, 64, 128), F32),
            VM((512, 512), BF16),
            VM((512, 256), F32),
            VM((32, 16, 256), F32),
        ],
    )
    delivered = exchange(returned, "tm")
    prior = call(
        rows_back_kernel,
        "vwl",
        (returned_rows.reshape(2048, 128), turn_v, behind),
        [((32, 8192), F32)],
        [VM((1024, 256), F32), half],
    )
    return call(final_kernel, "svv", (asked, delivered, prior), [((32, 8192), F32)])


def solution(mesh):
    return jax.shard_map(
        local,
        mesh=mesh,
        in_specs=(
            P("det", "tm"),
            P(("det", "tm"), None),
            P("det", "tm"),
            P(("det", "tm"), None),
            P(("det", "tm")),
            P(),
            P("det", None),
            P("det", None),
            P(),
        ),
        out_specs=P(("det", "tm"), None),
        check_vma=False,
    )
```

```python
import math

import jax
import jax.numpy as jnp
import numpy as np
from jax import lax
from jax.experimental import pallas as pl
from jax.experimental.pallas import tpu as pltpu
from jax.sharding import PartitionSpec as P


NBAND = 32
F32 = jnp.float32
BF16 = jnp.bfloat16
VM = pltpu.VMEM


def halves(table):
    high = np.asarray(table, np.float32).astype(BF16)
    low = (np.asarray(table, np.float64) - high.astype(np.float64)).astype(BF16)
    return high, low


def wave(rows, cols, period):
    turn = 2.0 * math.pi * ((rows[:, None] * cols[None, :]) % period) / period
    return np.cos(turn), np.sin(turn)


def stage_tables(width, copies):
    index = np.arange(width, dtype=np.float64)
    cos, sin = wave(index, index, width)
    half_cos, half_sin = wave(index, index + 0.5, width)
    eye = np.eye(copies)
    cos, sin = np.kron(eye, cos), np.kron(eye, sin)
    cas_half = np.kron(eye, half_cos + half_sin)
    zero = np.zeros_like(cos)
    general = np.block([[cos, -sin], [sin, cos]])
    special = np.block([[cos + sin, zero], [zero, cas_half]])
    return general, special


def row_tables():
    general, special = stage_tables(128, 1)
    return general, special


def twiddles(first, second, length):
    return [
        np.asarray(t, np.float32)
        for t in wave(np.arange(first, dtype=np.float64), second.astype(np.float64), length)
    ]


def band_tables():
    second = np.arange(128)
    general = np.minimum(np.minimum(second, 127 - second) // 2, NBAND - 1)
    special = np.minimum(np.minimum(second, 128 - second) // 2, NBAND - 1)
    bands = np.arange(NBAND)[:, None]
    return (bands == general[None]).astype(np.float32), (bands == special[None]).astype(np.float32)


def turn_by(pair, quotient, count, sign):
    real, imag = pair
    cos = math.cos(2.0 * math.pi * quotient / count)
    sin = sign * math.sin(2.0 * math.pi * quotient / count)
    if 8 * quotient == count:
        scale = math.sqrt(0.5)
        if sign < 0:
            return (real + imag) * scale, (imag - real) * scale
        return (real - imag) * scale, (imag + real) * scale
    return real * cos - imag * sin, real * sin + imag * cos


def real_transform(values):
    count = len(values)
    if count == 1:
        return [(values[0], None)]
    if count == 2:
        return [(values[0] + values[1], None), (values[0] - values[1], None)]
    even = real_transform(values[0::2])
    odd = real_transform(values[1::2])
    half = count // 2
    out = [None] * (half + 1)
    out[0] = (even[0][0] + odd[0][0], None)
    out[half] = (even[0][0] - odd[0][0], None)
    for k in range(1, half // 2):
        turned = turn_by(odd[k], k, count, -1.0)
        out[k] = (even[k][0] + turned[0], even[k][1] + turned[1])
        out[half - k] = (even[k][0] - turned[0], turned[1] - even[k][1])
    out[half // 2] = (even[half // 2][0], -odd[half // 2][0])
    return out


def real_inverse(spectrum, count):
    if count == 1:
        return [spectrum[0][0]]
    first, last = spectrum[0][0], spectrum[count // 2][0]
    if count == 2:
        return [first + last, first - last]
    half = count // 2
    even = [None] * (half // 2 + 1)
    odd = [None] * (half // 2 + 1)
    even[0] = (first + last, None)
    odd[0] = (first - last, None)
    for k in range(1, half // 2):
        one, two = spectrum[k], spectrum[half - k]
        even[k] = (one[0] + two[0], one[1] - two[1])
        odd[k] = turn_by((one[0] - two[0], one[1] + two[1]), k, count, 1.0)
    middle = spectrum[half // 2]
    even[half // 2] = (middle[0] + middle[0], None)
    odd[half // 2] = (-(middle[1] + middle[1]), None)
    out = [None] * count
    out[0::2] = real_inverse(even, half)
    out[1::2] = real_inverse(odd, half)
    return out


def forward_tile(values, cos_ref, sin_ref, store):
    half = len(values) // 2
    spectrum = real_transform(values)
    store(0, spectrum[0][0], spectrum[half][0])
    for k in range(1, half):
        real, imag = spectrum[k]
        cos, sin = cos_ref[k : k + 1, :], sin_ref[k : k + 1, :]
        store(k, real * cos + imag * sin, imag * cos - real * sin)


def inverse_tile(load, cos_ref, sin_ref, half=32):
    first, last = load(0)
    spectrum = [(first, None)]
    for k in range(1, half):
        real, imag = load(k)
        cos, sin = cos_ref[k : k + 1, :], sin_ref[k : k + 1, :]
        spectrum.append((real * cos - imag * sin, imag * cos + real * sin))
    spectrum.append((last, None))
    return real_inverse(spectrum, 2 * half)


def parts(value):
    high = value.astype(BF16)
    return high, (value - high.astype(F32)).astype(BF16)


def mm(left, right):
    return jnp.dot(left, right, preferred_element_type=F32)


def mm_right(value, high, low):
    top, rest = parts(value)
    return mm(top, high) + mm(rest, high) + mm(top, low)


def mm_left(high, low, value):
    top, rest = parts(value)
    return mm(high, top) + mm(high, rest) + mm(low, top)


def mm_both(left, right):
    high, low = parts(right)
    return mm_right(left, high, low)


def aligned(index, size):
    return pl.ds(pl.multiple_of(index * size, size), size)


def ids_kernel(owner, block, sky_hbm, send, slots, sky, counts, sem):
    copy = pltpu.make_async_copy(sky_hbm, sky, sem)
    copy.start()
    for i in range(16):
        counts[i] = 0
    row = lax.broadcasted_iota(jnp.int32, (16, 128), 0)
    lane = lax.broadcasted_iota(jnp.int32, (16, 128), 1)
    table = jnp.full((16, 128), 64, jnp.int32)
    for i in range(16):
        target = owner[i]
        place = counts[target]
        counts[target] = place + 1
        slots[i] = target * 2 + place
        table = jnp.where((row == target) & (lane == place), block[i], table)
    send[...] = table
    copy.wait()


def pick_kernel(asked, sky, out, sem):
    copies = []
    for i in range(32):
        block = jnp.minimum(asked[i // 2, i % 2], 63)
        copies.append(pltpu.make_async_copy(sky.at[:, aligned(block, 128)], out.at[i], sem.at[i]))
        copies[-1].start()
    for copy in copies:
        copy.wait()


def exact(source, onehot):
    return jnp.dot(
        source, onehot, precision=lax.Precision.HIGHEST, preferred_element_type=F32
    )


def level_weights(inv_white, bands):
    levels = inv_white[...].T
    return exact(levels, bands[0]), exact(levels, bands[1])


def point_pairs(pointing, turned):
    wide = jnp.concatenate([pointing[...], pointing[...]], axis=0)
    turned[...] = jnp.concatenate([wide, wide], axis=1).T
    lane = lax.broadcasted_iota(jnp.int32, (32, 128), 1)
    even, odd = turned[pl.ds(0, 32, stride=2), :], turned[pl.ds(1, 32, stride=2), :]
    return jnp.where(lane < 64, even, odd)


def rows_kernel(sky, turn, later, out, work, done):
    def tile(i, carry):
        rows = aligned(i, 8)
        values = [sky[rows, 128 * u : 128 * u + 128] for u in range(64)]

        def store(k, real, imag):
            work[k, rows, 0:128] = real
            work[k, rows, 128:256] = imag

        forward_tile(values, turn[0], turn[1], store)
        return carry

    lax.fori_loop(0, 4, tile, 0)
    tables = later.wait()
    for q in range(2):
        chunk = work[16 * q : 16 * q + 16].reshape(512, 256)
        done[512 * q : 512 * q + 512] = mm_right(chunk, tables[0], tables[1])
    done[0:32] = mm_right(work[0], tables[2], tables[3])
    for t in range(8):
        for c in range(2):
            block = done[128 * t : 128 * t + 128, 128 * c : 128 * c + 128]
            out[pl.ds(8 * c + t, 128, stride=16), :] = block.T


def columns_kernel(meta, data, turn, tables, out_hbm, work, gained, out, sems):
    def ahead(i, carry):
        tiles = aligned(i, 8)

        def store(k, real, imag):
            work[k, tiles, 0:128] = real
            work[k, tiles, 128:256] = imag

        forward_tile([data[d, tiles, :] for d in range(128)], turn[0], turn[1], store)
        return carry

    lax.fori_loop(0, 2, ahead, 0)
    total_rows, total_cols = 4096, 8192
    tile = lax.broadcasted_iota(jnp.int32, (16, 128), 0)
    lane = lax.broadcasted_iota(jnp.int32, (16, 128), 1)
    first = 4 * (tile % 8) + lane // 32
    first = jnp.where((first == 0) & (tile == 8), 32, first)
    horizontal = meta[1] * 64 + first
    lane_row = lax.broadcasted_iota(jnp.int32, (1, 128), 1)
    folded = jnp.minimum(horizontal, total_cols - horizontal).astype(F32) / total_cols
    across = folded * folded
    knee_sq = 1.0 / (2.0 * math.pi * (total_rows / 64.0)) ** 2

    def middle(q, carry):
        chunk = work[aligned(q, 16)].reshape(256, 256)
        gained[aligned(q, 16)] = mm_right(chunk, tables[0], tables[1]).reshape(16, 16, 256)

        @pl.when(q == 0)
        def _():
            gained[0] = mm_right(work[0], tables[2], tables[3])

        for j in range(16):
            k = 16 * q + j
            for part in range(2):
                lead = jnp.where((k == 0) & (part == 1), 64, k)
                vertical = lead + 128 * (lane_row % 32)
                fold = jnp.minimum(vertical, total_rows - vertical).astype(F32) / total_rows
                radial = fold * fold + across
                gain = 1.0 + radial * (1.0 / 0.05) + 0.25 * lax.rsqrt(radial + knee_sq)
                lanes = slice(128 * part, 128 * part + 128)
                gained[k, :, lanes] = gained[k, :, lanes] * (-gain)
        chunk = gained[aligned(q, 16)].reshape(256, 256)
        work[aligned(q, 16)] = mm_right(chunk, tables[4], tables[5]).reshape(16, 16, 256)

        @pl.when(q == 0)
        def _():
            work[0] = mm_right(gained[0], tables[6], tables[7])

        return carry

    lax.fori_loop(0, 4, middle, 0)

    def outward(i):
        return pltpu.make_async_copy(out.at[i], out_hbm.at[:, aligned(i, 8)], sems.at[i])

    def behind(i, carry):
        tiles = aligned(i, 8)

        def load(k):
            return work[k, tiles, 0:128], work[k, tiles, 128:256]

        values = inverse_tile(load, turn[0], turn[1], 64)
        for d in range(128):
            out[i, d] = values[d]
        outward(i).start()
        return carry

    lax.fori_loop(0, 2, behind, 0)
    for i in range(2):
        outward(i).wait()


def rows_back_kernel(data, turn, later, out, work, done):
    for t in range(8):
        for c in range(2):
            block = data[pl.ds(8 * c + t, 128, stride=16), :]
            work[128 * t : 128 * t + 128, 128 * c : 128 * c + 128] = block.T
    tables = later.wait()
    for q in range(2):
        chunk = work[512 * q : 512 * q + 512]
        done[16 * q : 16 * q + 16] = mm_right(chunk, tables[0], tables[1]).reshape(16, 32, 256)
    done[0] = mm_right(work[0:32], tables[2], tables[3])

    def tile(i, carry):
        rows = aligned(i, 8)

        def load(k):
            return done[k, rows, 0:128], done[k, rows, 128:256]

        values = inverse_tile(load, turn[0], turn[1])
        for u in range(64):
            out[rows, 128 * u : 128 * u + 128] = values[u]
        return carry

    lax.fori_loop(0, 4, tile, 0)


def stage_kernel(
    inv_white, bands, loading_t, kernel, pointing, *refs
):
    sources, targets = refs[:5], refs[5:10]
    weights, couple, mixing, pairs, turned, sems = refs[10:]
    copies = [pltpu.make_async_copy(a, b, sems.at[n]) for n, (a, b) in enumerate(zip(sources, targets))]
    for copy in copies:
        copy.start()
    weights[0], weights[1] = level_weights(inv_white, bands)
    for part in range(2):
        couple[part] = exact(kernel[...], bands[part])
    mixing[...] = loading_t[...].T
    pairs[...] = point_pairs(pointing, turned)
    for copy in copies:
        copy.wait()


def detect_kernel(
    meta, slots, pointing, data_later, arrived, beam, turn, tables, weights, loading_t, spectrum_hbm, mine,
    theirs, points, picked, table, onehot, signal, work, spectrum, sems,
):
    weight, weight_zero = weights[0], weights[1]
    for i in range(16):
        picked[32 * i : 32 * i + 32] = arrived[slots[i]]
    high, low = parts(mm_both(picked[...], beam[...].T))
    table[:, 0:128] = high
    table[:, 128:256] = low
    points[:, 0:64] = pointing[...]
    points[:, 64:128] = pointing[...]
    lane = lax.broadcasted_iota(jnp.int32, (64, 512), 1)

    def gather(c, carry):
        moved = pltpu.roll(points[...], (128 - 8 * c) % 128, 1)
        for u in range(8):
            hit = moved[:, u : u + 1] == lane
            onehot[64 * u : 64 * u + 64] = jnp.where(hit, 1.0, 0.0).astype(BF16)
        both = mm(onehot[...], table[...])
        signal[aligned(c, 8)] = (both[:, 0:128] + both[:, 128:256]).reshape(8, 64, 128)
        return carry

    lax.fori_loop(0, 8, gather, 0)
    data = data_later.wait()

    def tile(i, carry):
        rows = aligned(i, 8)
        values = [data[rows, 128 * u : 128 * u + 128] - signal[u, rows, :] for u in range(64)]

        def store(k, real, imag):
            work[k, rows, 0:128] = real
            work[k, rows, 128:256] = imag

        forward_tile(values, turn[0], turn[1], store)
        return carry

    lax.fori_loop(0, 8, tile, 0)

    def outward(q):
        rows = aligned(q, 8)
        return pltpu.make_async_copy(spectrum.at[rows], spectrum_hbm.at[rows], sems.at[q])

    def stage(q, carry):
        chunk = work[aligned(q, 8)].reshape(512, 256)
        spectrum[aligned(q, 8)] = mm_right(chunk, tables[0], tables[1]).reshape(8, 64, 256)

        @pl.when(q == 0)
        def _():
            spectrum[0] = mm_right(work[0], tables[2], tables[3])

        outward(q).start()
        return carry

    lax.fori_loop(0, 4, stage, 0)
    left_h, left_l = parts(loading_t[...])
    core = meta[3]

    def project(i, carry):
        for out, side in ((theirs, 1 - core), (mine, core)):
            k = 8 * (i // 4) + 4 * side + i % 4
            first = jnp.where(k == 0, weight_zero, weight)
            scale = jnp.concatenate([first, weight], axis=1)
            out[i] = mm_left(left_h, left_l, spectrum[k] * scale)
        return carry

    lax.fori_loop(0, 16, project, 0, unroll=4)
    for q in range(4):
        outward(q).wait()


def merge_kernel(meta, mine, theirs, *outs):
    for s in range(4):
        rows = aligned((meta[2] + s) % 4, 4)
        outs[s][...] = mine[rows] + theirs[rows]


def couple_kernel(meta, own, one, two, three, couple, out):
    for k in range(4):
        total = (own[k] + one[k]) + (two[k] + three[k])
        real = jnp.zeros((16, 128), F32)
        imag = jnp.zeros((16, 128), F32)
        for n in range(16):
            factor = couple[0, pl.ds(n, 16, stride=16), :]
            first = factor
            if k == 0:
                first = jnp.where(meta[0] == 0, couple[1, pl.ds(n, 16, stride=16), :], factor)
            real = real + first * total[n : n + 1, 0:128]
            imag = imag + factor * total[n : n + 1, 128:256]
        out[k, :, 0:128] = real
        out[k, :, 128:256] = imag


def clean_kernel(
    meta, slots, pairs, a0, a1, a2, a3, b0, b1, b2, b3, spectrum_later, weights, mixing, beam, turn,
    tables_later, out, filtered, work, cleaned, onehot, total, coupled,
):
    for s, (here, there) in enumerate(((a0, b0), (a1, b1), (a2, b2), (a3, b3))):
        chip = (meta[2] + (4 - s)) % 4
        coupled[aligned(2 * chip + meta[3], 4)] = here[...]
        coupled[aligned(2 * chip + 1 - meta[3], 4)] = there[...]
    left_h, left_l = parts(mixing[...])
    weight, weight_zero = weights[0], weights[1]

    def remove(k, carry):
        first = jnp.where(k == 0, weight_zero, weight)
        scale = jnp.concatenate([first, weight], axis=1)
        filtered[k] = scale * (spectrum[k] - mm_left(left_h, left_l, coupled[k]))
        return carry

    spectrum = spectrum_later.wait()
    lax.fori_loop(0, 32, remove, 0, unroll=4)
    tables = tables_later.wait()

    def stage(q, carry):
        chunk = filtered[aligned(q, 8)].reshape(512, 256)
        work[aligned(q, 8)] = mm_right(chunk, tables[0], tables[1]).reshape(8, 64, 256)
        return carry

    lax.fori_loop(0, 4, stage, 0)
    work[0] = mm_right(filtered[0], tables[2], tables[3])

    def tile(i, carry):
        rows = aligned(i, 8)

        def load(k):
            return work[k, rows, 0:128], work[k, rows, 128:256]

        values = inverse_tile(load, turn[0], turn[1])
        for u in range(64):
            cleaned[u, rows, :] = values[u]
        return carry

    lax.fori_loop(0, 8, tile, 0)
    sub = lax.broadcasted_iota(jnp.int32, (512, 128), 0)
    total[...] = jnp.zeros((512, 256), F32)

    def scatter(c, carry):
        for u in range(4):
            hit = pairs[pl.ds(4 * c + u, 1), :] == sub
            onehot[:, 128 * u : 128 * u + 128] = jnp.where(hit, 1.0, 0.0).astype(BF16)
        high, low = parts(cleaned[aligned(c, 8)].reshape(512, 128))
        total[...] += mm(onehot[...], jnp.concatenate([high, low], axis=1))
        return carry

    lax.fori_loop(0, 8, scatter, 0)
    summed = total[:, 0:128] + total[:, 128:256]
    grads = mm_both(summed, beam[...])
    out[...] = jnp.zeros((32, 32, 128), F32)
    for i in range(16):
        out[slots[i]] = grads[32 * i : 32 * i + 32]


def final_kernel(asked, delivered, prior, out):
    out[...] = prior[...]

    def step(i, carry):
        for c in range(2):
            block = asked[i, c]

            @pl.when(block < 64)
            def _():
                lanes = aligned(block, 128)
                out[:, lanes] = out[:, lanes] + delivered[2 * i + c]

        return carry

    lax.fori_loop(0, 16, step, 0)


SM = pltpu.SMEM
HBM = pltpu.HBM
DMA = pltpu.SemaphoreType.DMA
KEEP = "keep"


class Later:
    def __init__(self, ref, copy):
        self.ref, self.copy = ref, copy

    def wait(self):
        self.copy.wait()
        return self.ref


def call(kernel, modes, ins, outs, scratch=(), out_spaces=None, limit=24):
    count, moved = len(ins), [i for i, m in enumerate(modes) if m in "etl"]
    spaces = {"v": VM, "w": VM, "s": SM}
    in_specs = [pl.BlockSpec(memory_space=spaces.get(m, HBM)) for m in modes]
    out_specs = [
        pl.BlockSpec(memory_space=VM if s is KEEP else s) for s in (out_spaces or [VM] * len(outs))
    ]
    far = out_spaces or [VM] * len(outs)
    shapes = [
        (VM if f is KEEP else HBM)(s, d) if f in (HBM, KEEP) else jax.ShapeDtypeStruct(s, d)
        for (s, d), f in zip(outs, far)
    ]
    buffers = [(SM if modes[i] == "t" else VM)(ins[i].shape, ins[i].dtype) for i in moved]

    def body(*refs):
        refs = list(refs)
        if moved:
            sems, targets = refs[-1], refs[-1 - len(moved) : -1]
            copies = []
            for n, (i, target) in enumerate(zip(moved, targets)):
                copies.append(pltpu.make_async_copy(refs[i], target, sems.at[n]))
            for kind in ("et", "l"):
                for i, copy in zip(moved, copies):
                    if modes[i] in kind:
                        copy.start()
            for i, target, copy in zip(moved, targets, copies):
                if modes[i] == "l":
                    refs[i] = Later(target, copy)
                else:
                    copy.wait()
                    refs[i] = target
            refs = refs[: -1 - len(moved)]
        kernel(*refs)

    run = pl.pallas_call(
        body,
        out_shape=shapes,
        in_specs=in_specs,
        out_specs=out_specs,
        scratch_shapes=list(scratch) + (buffers + [DMA((len(moved),))] if moved else []),
        compiler_params=pltpu.CompilerParams(vmem_limit_bytes=limit * 1024 * 1024),
    )
    assert len(modes) == count
    ins = [
        pltpu.with_memory_space_constraint(x, VM if m == "w" else HBM) if m in "hetlw" else x
        for x, m in zip(ins, modes)
    ]
    result = run(*ins)
    return result if len(outs) > 1 else result[0]


def row_constants():
    general, special = row_tables()
    turn = np.stack(twiddles(32, np.arange(128), 8192))
    scale = 2.0**-13
    ahead = np.stack([*halves(general), *halves(special)])
    behind = np.stack([*halves(general.T * scale), *halves(special.T * scale)])
    return turn, ahead, behind


def col_constants():
    general, special = stage_tables(32, 4)
    turn = np.stack(twiddles(64, np.arange(128) % 32, 4096))
    scale = 2.0**-12
    behind = (*halves(general.T * scale), *halves(special.T * scale))
    return turn, np.stack([*halves(general), *halves(special), *behind])


def exchange(value, axes):
    return lax.all_to_all(value, axes, split_axis=0, concat_axis=0, tiled=True)


def core_swap(value):
    return lax.ppermute(value, "det", [(g, g ^ 1) for g in range(8)])


def chip_shift(value, step):
    return lax.ppermute(value, "det", [(g, (g + 2 * step) % 8) for g in range(8)])


def local(
    detector_data,
    sky_map,
    pointing,
    request_owner,
    request_block,
    beam_kernel,
    inv_white,
    mode_loading,
    mode_kernel,
):
    turn, ahead, behind = (jnp.asarray(t) for t in row_constants())
    col_turn, tables = (jnp.asarray(t) for t in col_constants())
    bands = jnp.asarray(np.stack(band_tables()))
    det = lax.axis_index("det").astype(jnp.int32)
    rank = det * lax.axis_size("tm") + lax.axis_index("tm").astype(jnp.int32)
    meta = jnp.stack([det, rank, det // 2, det % 2])
    square, half = VM((32, 64, 256), F32), VM((32, 32, 256), F32)
    flat = (32, 32, 128)
    loading_t, inv_white = mode_loading.T, inv_white.T

    send, slots, sky_v = call(
        ids_kernel,
        "tth",
        (request_owner.reshape(16), request_block, sky_map),
        [((16, 128), jnp.int32), ((16,), jnp.int32), ((32, 8192), F32)],
        [SM((16,), jnp.int32), DMA],
        [VM, SM, KEEP],
    )
    asked = exchange(send, "tm")
    outgoing = call(pick_kernel, "sw", (asked, sky_v), [(flat, F32)], [DMA((32,))], [HBM])
    arrived = exchange(outgoing, "tm")

    wide = ((2048, 128), F32)
    packed = call(
        rows_kernel, "wel", (sky_v, turn, ahead), [wide], [half, VM((1024, 256), F32)]
    )
    columns = exchange(packed.reshape(128, 16, 128), ("det", "tm"))

    moved = (turn, ahead, beam_kernel, col_turn, tables)
    turn_v, ahead_v, beam_v, col_turn_v, tables_v, weights, couple, mixing, pairs = call(
        stage_kernel,
        "eeeeehhhhh",
        (
            inv_white, bands, loading_t, mode_kernel.transpose(1, 2, 0).reshape(256, NBAND), pointing,
            *moved,
        ),
        [(m.shape, m.dtype) for m in moved]
        + [
            ((2, 64, 128), F32),
            ((2, 256, 128), F32),
            ((64, 16), F32),
            ((32, 128), jnp.int32),
        ],
        [VM((128, 128), jnp.int32), DMA((5,))],
        [KEEP] * 9,
    )
    spectrum, mine, theirs = call(
        detect_kernel,
        "sselvwwwwe",
        (meta, slots, pointing, detector_data, arrived, beam_v, turn_v, ahead_v, weights, loading_t),
        [((32, 64, 256), F32), ((16, 16, 256), F32), ((16, 16, 256), F32)],
        [
            VM((64, 128), jnp.int32),
            VM((512, 128), F32),
            VM((512, 256), BF16),
            VM((512, 512), BF16),
            VM((64, 64, 128), F32),
            square,
            square,
            DMA((4,)),
        ],
        [HBM, VM, VM],
    )
    share = ((4, 16, 256), F32)
    partner = core_swap(theirs)
    sums = call(merge_kernel, "svv", (meta, mine, partner), [share] * 4)
    gathered = [sums[0]] + [chip_shift(sums[s], s) for s in range(1, 4)]
    coupled = call(couple_kernel, "svvvvw", (meta, *gathered, couple), [share])
    here = [coupled] + [chip_shift(coupled, s) for s in range(1, 4)]
    there = [core_swap(value) for value in here]

    filtered = call(
        columns_kernel,
        "svww",
        (meta, columns, col_turn_v, tables_v),
        [((128, 16, 128), F32)],
        [VM((64, 16, 256), F32), VM((64, 16, 256), F32), VM((2, 128, 8, 128), F32), DMA((2,))],
        [HBM],
    )
    returned_rows = exchange(filtered, ("det", "tm"))

    returned = call(
        clean_kernel,
        "ssw" + "v" * 8 + "lwwwwl",
        (meta, slots, pairs, *here, *there, spectrum, weights, mixing, beam_v, turn_v, behind),
        [(flat, F32)],
        [
            square,
            square,
            VM((64, 64, 128), F32),
            VM((512, 512), BF16),
            VM((512, 256), F32),
            VM((32, 16, 256), F32),
        ],
    )
    delivered = exchange(returned, "tm")
    prior = call(
        rows_back_kernel,
        "vwl",
        (returned_rows.reshape(2048, 128), turn_v, behind),
        [((32, 8192), F32)],
        [VM((1024, 256), F32), half],
    )
    return call(final_kernel, "svv", (asked, delivered, prior), [((32, 8192), F32)])


def solution(mesh):
    return jax.shard_map(
        local,
        mesh=mesh,
        in_specs=(
            P("det", "tm"),
            P(("det", "tm"), None),
            P("det", "tm"),
            P(("det", "tm"), None),
            P(("det", "tm")),
            P(),
            P("det", None),
            P("det", None),
            P(),
        ),
        out_specs=P(("det", "tm"), None),
        check_vma=False,
    )
```
